512 devices in a mesh: req: 64 (over x, y, core), tp: 8 (over z).
Axes of the slice: x: 4, y: 8, z: 8, core: 2. Of those that a mesh axis runs over, the one named last changes fastest.
Arguments:
- queries: bfloat16 [64, 28, 4096], P('req', None, 'tp'), may hold values from -25 to 25
- tree_kv: bfloat16 [64, 28, 2048], P('req', None, 'tp'), may hold values from -4 to 4
- tree_parent: int32 [64, 28], P('req'), may hold values from -1 to 26, as said below
- accepted_path: int32 [64, 8], replicated, may hold values from -1 to 27, as said below
- cache_kv: bfloat16 [192, 256, 2048], P('req', None, 'tp'), may hold values from -6 to 6
- piece_owner: int32 [192, 2], P('req'), may hold values from -1 to 63, as said below
- cache_len: int32 [64], replicated, may hold values from 1 to 1016, as said below
- out_weight: bfloat16 [4096, 4096], P('tp', 'req'), may hold values from -0.09375 to 0.09375
Outputs:
- mixed: bfloat16 [64, 28, 4096], P('tp', None, 'req')
- cache_out: bfloat16 [192, 256, 2048], P('req', None, 'tp')
The draws below stay inside these ranges and needn't reach their ends.
Inputs may be any that keep to these rules, and one draw needn't show every extreme that they name: tree_parent[r, 0] = -1 and 0 <= tree_parent[r, i] < i for i >= 1; tokens 1 to 7 have parent i - 1. accepted_path[r] lists, root first, the tokens on the path from token 0 to some token of request r's tree, then -1 entries; it holds 1 to 8 tokens, and 8 for some request. piece_owner[s] = (r, p) means slot s holds cache rows p * 256 to p * 256 + 255 of request r; (-1, -1) marks an unused slot. For each request r the pieces 0 to (cache_len[r] + 7) // 256 stand in exactly one slot each, and no other pieces do. cache_len[r] + 8 <= 1024.
All inputs are finite; a program needn't handle non-finite values.
Results may differ from the reference program's by a relative error of at most 0.02.
Values may be sent and summed in bfloat16 or wider, within the bound.
No kernel may reach another device: no remote copies, remote signals or barrier semaphores. Data moves between devices by JAX's collectives and lax.ppermute only.
A program may use at most 64 MiB of HBM per device.

```python
import math
import jax
import jax.numpy as jnp
from jax import lax

D = 4096
H = 32
KVH = 8
HD = 128
TREE = 28
DEPTH = 8
PIECE = 256
MAXP = 4
REQS = 64
SLOTS = 192


def attention_inputs(key):
    base_key = jax.random.fold_in(key, 11)
    key_query, key_rows = jax.random.split(base_key, 2)
    query_vals = jax.random.truncated_normal(key_query, -4.0, 4.0, (REQS, TREE, H, HD), jnp.float32)
    tree_rows = jax.random.truncated_normal(key_rows, -4.0, 4.0, (REQS, TREE, KVH, 2, HD), jnp.float32)
    return (query_vals.reshape(REQS, TREE, H * HD), tree_rows.reshape(REQS, TREE, KVH * 2 * HD))


def tree_shape(key):
    base_key = jax.random.fold_in(key, 23)
    key_parent, key_pick, key_forced = jax.random.split(base_key, 3)
    node_ids = jnp.arange(TREE, dtype=jnp.int32)
    request_ids = jnp.arange(REQS, dtype=jnp.int32)
    forced = jax.random.randint(key_forced, (), 0, REQS)
    second = (forced + 1) % REQS
    raw_ints = jax.random.randint(key_parent, (REQS, TREE), 0, 1 << 20)
    parent = raw_ints % jnp.maximum(node_ids, 1)[None, :]
    parent = jnp.where(node_ids[None, :] < DEPTH, node_ids[None, :] - 1, parent).astype(jnp.int32)
    is_second = (request_ids == second)[:, None]
    parent = jnp.where(is_second & (node_ids[None, :] == TREE - 2), 0, parent)
    parent = jnp.where(is_second & (node_ids[None, :] == TREE - 1), TREE - 2, parent).astype(jnp.int32)
    depths = jnp.zeros((REQS, TREE), jnp.int32)
    for rounds in range(TREE):
        above = jnp.take_along_axis(depths, jnp.maximum(parent, 0), axis=1)
        depths = jnp.where(node_ids[None, :] > 0, above + 1, 0)
    scores = jax.random.randint(key_pick, (REQS, TREE), 0, 1 << 20) * TREE + node_ids[None, :]
    scores = jnp.where(depths < DEPTH, scores, -1)
    target = jnp.argmax(scores, axis=1).astype(jnp.int32)
    target = jnp.where(request_ids == forced, DEPTH - 1, target).astype(jnp.int32)
    target = jnp.where(request_ids == second, TREE - 1, target).astype(jnp.int32)
    target_depth = jnp.take_along_axis(depths, target[:, None], axis=1)[:, 0]
    path = jnp.full((REQS, DEPTH + 1), -1, jnp.int32)
    current = target
    for stepping in range(DEPTH):
        valid = stepping <= target_depth
        column = jnp.where(valid, target_depth - stepping, DEPTH)
        path = path.at[request_ids, column].set(jnp.where(valid, current, -1))
        upward = jnp.take_along_axis(parent, current[:, None], axis=1)[:, 0]
        current = jnp.where(current > 0, upward, 0).astype(jnp.int32)
    return (parent, path[:, :DEPTH])


def cache_layout(key):
    base_key = jax.random.fold_in(key, 37)
    key_count, key_pair, key_rest, key_forced, key_perm = jax.random.split(base_key, 5)
    half_reqs = REQS // 2
    order = jax.random.permutation(key_pair, REQS)
    first = jax.random.randint(key_count, (half_reqs,), 1, MAXP + 1)
    forced = jax.random.randint(key_forced, (), 0, half_reqs)
    first = jnp.where(jnp.arange(half_reqs) == forced, MAXP, first)
    paired = jnp.concatenate([first, MAXP + 1 - first]).astype(jnp.int32)
    pieces = jnp.zeros((REQS,), jnp.int32).at[order].set(paired)
    remainder = jax.random.randint(key_rest, (REQS,), 1, PIECE - DEPTH + 1)
    remainder = jnp.where(jnp.arange(REQS) == order[forced], PIECE - DEPTH, remainder)
    lengths = ((pieces - 1) * PIECE + remainder).astype(jnp.int32)
    ends = jnp.cumsum(pieces).astype(jnp.int32)
    starts = ends - pieces
    total = half_reqs * (MAXP + 1)
    global_ids = jnp.arange(SLOTS, dtype=jnp.int32)
    owner_req = jnp.sum((ends[None, :] <= global_ids[:, None]).astype(jnp.int32), axis=1)
    safe_req = jnp.minimum(owner_req, REQS - 1)
    owner_piece = global_ids - starts[safe_req]
    live = global_ids < total
    entries = jnp.stack([jnp.where(live, owner_req, -1), jnp.where(live, owner_piece, -1)], axis=1).astype(jnp.int32)
    shuffle = jax.random.permutation(key_perm, SLOTS)
    owners = jnp.full((SLOTS, 2), -1, jnp.int32).at[shuffle].set(entries)
    return (lengths, owners)


def draw_queries(key, part):
    return attention_inputs(key)[0].astype(jnp.bfloat16)


def draw_tree_kv(key, part):
    return attention_inputs(key)[1].astype(jnp.bfloat16)


def draw_tree_parent(key, part):
    return tree_shape(key)[0]


def draw_accepted_path(key, part):
    return tree_shape(key)[1]


def draw_cache_len(key, part):
    return cache_layout(key)[0]


def draw_piece_owner(key, part):
    return cache_layout(key)[1]


def level_of(key, dims, cuts, smallest, largest):
    level = 1.0
    for position, blocks in cuts:
        heights = jax.random.uniform(jax.random.fold_in(jax.random.fold_in(key, 6), position), (blocks,), jnp.float32, smallest / len(cuts), largest / len(cuts))
        level = level * jnp.repeat(jnp.exp(heights), dims[position] // blocks).reshape((-1,) + (1,) * (len(dims) - 1 - position))
    return level


def scatter_about(own_key, extent, scale, bound, cuts=(), held_as=jnp.bfloat16):
    values = scale * jax.random.normal(own_key, extent, jnp.float32)
    if cuts:
        values = values * level_of(own_key, extent, cuts, -0.22, 0.18)
    return jnp.clip(values, -bound, bound).astype(held_as)


def setup_inputs(seed: int = 0) -> dict:
    arg_keys = jax.random.split(jax.random.key(seed), 9)
    return {
        "queries": draw_queries(jax.random.fold_in(arg_keys[8], 71), 0),
        "tree_kv": draw_tree_kv(jax.random.fold_in(arg_keys[8], 71), 0),
        "tree_parent": draw_tree_parent(jax.random.fold_in(arg_keys[8], 71), 0),
        "accepted_path": draw_accepted_path(jax.random.fold_in(arg_keys[8], 71), 0),
        "cache_kv": scatter_about(arg_keys[4], (SLOTS, PIECE, KVH * 2 * HD), 1.0, 6.0, ((0, 64), (2, 8))),
        "piece_owner": draw_piece_owner(jax.random.fold_in(arg_keys[8], 71), 0),
        "cache_len": draw_cache_len(jax.random.fold_in(arg_keys[8], 71), 0),
        "out_weight": scatter_about(arg_keys[7], (H * HD, D), (H * HD) ** -0.5, 0.09375, ((0, 8), (1, 64))),
    }


NEG = -1e+30

def ancestors(parent):
    tree_size = parent.shape[-1]
    node_ids = lax.broadcasted_iota(jnp.int32, (tree_size, tree_size), 1)
    parent_hot = (parent[..., :, None] == node_ids).astype(jnp.float32)
    reached = jnp.minimum(parent_hot + jnp.eye(tree_size, dtype=jnp.float32), 1.0)
    for rounds in range(max(1, (tree_size - 1).bit_length())):
        reached = jnp.minimum(jnp.einsum('rij,rjk->rik', reached, reached, precision=lax.Precision.HIGHEST), 1.0)
    return reached

def reference(queries, tree_kv, tree_parent, accepted_path, cache_kv, piece_owner, cache_len, out_weight):
    group_size = H // KVH
    scaling = 1.0 / math.sqrt(HD)
    reached = ancestors(tree_parent)
    slot_ids = jnp.arange(SLOTS, dtype=jnp.int32)
    owner_req = piece_owner[:, 0]
    owner_piece = piece_owner[:, 1]
    flat_index = jnp.where(owner_req >= 0, owner_req * MAXP + owner_piece, REQS * MAXP).astype(jnp.int32)
    table = jnp.zeros((REQS * MAXP + 1,), jnp.int32).at[flat_index].set(slot_ids)
    table = table[:REQS * MAXP].reshape(REQS, MAXP)
    position_ids = jnp.arange(MAXP * PIECE, dtype=jnp.int32)

    def one_request(request):
        gathered = jnp.take(cache_kv, table[request], axis=0).reshape(MAXP * PIECE, KVH, 2, HD).astype(jnp.float32)
        visible = position_ids < cache_len[request]
        query = queries[request].reshape(TREE, KVH, group_size, HD).astype(jnp.float32)
        fresh = tree_kv[request].reshape(TREE, KVH, 2, HD).astype(jnp.float32)
        cache_scores = jnp.einsum('ikgd,tkd->ikgt', query, gathered[:, :, 0]) * scaling
        cache_scores = jnp.where(visible, cache_scores, NEG)
        tree_mask = reached[request][:, None, None, :] > 0.5
        tree_scores = jnp.where(tree_mask, jnp.einsum('ikgd,jkd->ikgj', query, fresh[:, :, 0]) * scaling, NEG)
        peak = jnp.maximum(lax.optimization_barrier(jnp.max(cache_scores, -1)), lax.optimization_barrier(jnp.max(tree_scores, -1)))
        cache_exp = jnp.where(visible, jnp.exp(cache_scores - peak[..., None]), 0.0)
        tree_exp = jnp.where(tree_mask, jnp.exp(tree_scores - peak[..., None]), 0.0)
        denom = lax.optimization_barrier(jnp.sum(cache_exp, -1)) + lax.optimization_barrier(jnp.sum(tree_exp, -1))
        cache_weights = lax.optimization_barrier(cache_exp.astype(jnp.bfloat16)).astype(jnp.float32)
        tree_weights = lax.optimization_barrier(tree_exp.astype(jnp.bfloat16)).astype(jnp.float32)
        numer = jnp.einsum('ikgt,tkd->ikgd', cache_weights, gathered[:, :, 1])
        numer = numer + jnp.einsum('ikgj,jkd->ikgd', tree_weights, fresh[:, :, 1])
        return (numer / denom[..., None]).reshape(TREE, H * HD).astype(jnp.bfloat16)
    attention = lax.map(one_request, jnp.arange(REQS, dtype=jnp.int32))
    mixed = jnp.dot(attention.reshape(REQS * TREE, H * HD), out_weight, preferred_element_type=jnp.float32)
    mixed = mixed.astype(jnp.bfloat16).reshape(REQS, TREE, D)
    columns = KVH * 2 * HD
    counts = lax.optimization_barrier(jnp.sum((accepted_path >= 0).astype(jnp.int32), axis=1))
    offsets = jnp.arange(DEPTH, dtype=jnp.int32)
    positions = cache_len[:, None] + offsets[None, :]
    slot_of = jnp.take_along_axis(table, (positions // PIECE).astype(jnp.int32), axis=1)
    valid = offsets[None, :] < counts[:, None]
    target = jnp.where(valid, slot_of * PIECE + positions % PIECE, SLOTS * PIECE).astype(jnp.int32)
    new_rows = jnp.take_along_axis(tree_kv, jnp.maximum(accepted_path, 0)[:, :, None].astype(jnp.int32), axis=1)
    flat_cache = cache_kv.reshape(SLOTS * PIECE, columns)
    flat_cache = flat_cache.at[target.reshape(-1)].set(new_rows.reshape(REQS * DEPTH, columns), mode='drop')
    cache_out = flat_cache.reshape(SLOTS, PIECE, columns)
    return (mixed, cache_out)
```

```python
import functools
import math

import jax
import jax.numpy as jnp
from jax import lax
from jax.experimental import pallas as pl
from jax.experimental.pallas import tpu as pltpu
from jax.sharding import PartitionSpec as P

HD = 128
NEG = -1e30
TOK = 32
F32 = jnp.float32
BF16 = jnp.bfloat16


def iota(shape, dim):
    return lax.broadcasted_iota(jnp.int32, shape, dim)


def pack_body(owner, path, cache, tree, out):
    slots = cache.shape[0]
    own = lax.axis_index("req")
    for s in range(slots):
        out[0:32, s] = cache[s, :, 0:HD].reshape(32, 8, HD)
        out[32:64, s] = cache[s, :, HD : 2 * HD].reshape(32, 8, HD)
    lane = iota((8, HD), 1)
    row = iota((8, HD), 0)
    keys = jnp.full((8, HD), -1, jnp.int32)
    for s in range(slots):
        key = jnp.where(owner[s, 0] >= 0, owner[s, 0] * 4 + owner[s, 1], -1)
        keys = jnp.where(lane == s, key, keys)
    keyrow = jnp.where(row == 0, keys, 0).astype(F32)
    depth = path.shape[1]
    tokens = tree.shape[1]
    hot_col = iota((depth, tokens), 1)
    hot_row = iota((depth, tokens), 0)
    hot = jnp.zeros((depth, tokens), jnp.bool_)
    for d in range(depth):
        hot = hot | ((hot_row == d) & (hot_col == path[own, d]))
    rows = jnp.dot(hot.astype(BF16), tree[0], preferred_element_type=F32)
    zero = jnp.zeros((4, HD), F32)
    for h in range(4):
        chunk = rows[4 * (h % 2) : 4 * (h % 2) + 4, HD * (h // 2) : HD * (h // 2) + HD]
        tile = (jnp.concatenate([zero, chunk], axis=0) + keyrow).astype(BF16)
        for i in range(slots):
            out[4 * i + h, 3] = tile
    rest = keyrow.astype(BF16)
    for j in range(4 * slots, 64):
        out[j, 3] = rest


def route_body(got, out, table, table_s, sem):
    own = lax.axis_index("req")
    which = jnp.minimum(own // 4, 2)
    keys = got[:, 3, 0:1, :].astype(F32).reshape(64, HD)
    target = iota((64, 256), 1).astype(F32)
    source = iota((64, 256), 0).astype(F32)
    found = jnp.zeros((64, 256), F32)
    mine = jnp.zeros((64, 1), F32)
    for i in range(3):
        key = keys[:, i : i + 1]
        found = found + jnp.where(key == target, source * 4.0 + float(i), 0.0)
        mine = jnp.where(which == i, key, mine)
    holder = jnp.floor(jnp.maximum(mine, 0.0) * 0.25) * 4.0 + 3.0
    holder = jnp.sum(jnp.where(source == target, holder, 0.0), axis=0, keepdims=True)
    found = jnp.sum(found, axis=0, keepdims=True)
    table[...] = jnp.concatenate([found, holder], axis=0).astype(jnp.int32)
    copy = pltpu.make_async_copy(table, table_s, sem)
    copy.start()
    copy.wait()

    def step(r, carry):
        for p in range(4):
            t = table_s[0, 4 * r + p]
            out[r, p] = got[t // 4, t % 4]
        out[r, 4] = got[table_s[1, r] // 4, 3]
        return carry

    lax.fori_loop(0, 64, step, 0, unroll=4)


def closure(parent):
    n = TOK
    up = iota((n, n), 0)
    here = iota((n, n), 1)
    pad = jnp.concatenate([parent, jnp.full((1, n - parent.shape[1]), -1, jnp.int32)], axis=1)
    eye = (up == here).astype(F32)
    reach = jnp.minimum((up == pad).astype(F32) + eye, 1.0)
    for rounds in range(5):
        low = reach.astype(BF16)
        reach = jnp.minimum(jnp.dot(low, low, preferred_element_type=F32), 1.0)
    return lax.dot_general(
        reach.astype(BF16), eye.astype(BF16), (((0,), (0,)), ((), ())), preferred_element_type=F32
    )


def attend_body(lens, query, tree, parent, got, out, q_s, t_s):
    own = lax.axis_index("req")
    tokens = query.shape[1]
    length = lens[own]
    q_s[...] = jnp.zeros_like(q_s)
    t_s[...] = jnp.zeros_like(t_s)
    for g in range(4):
        q_s[g * TOK : g * TOK + tokens, :] = query[0, :, g * HD : (g + 1) * HD]
    t_s[0:tokens, :] = tree[0]
    q = q_s[...]
    scaling = 1.0 / math.sqrt(HD)
    dims = (((1,), (1,)), ((), ()))
    reached = closure(parent[...])
    tree_mask = jnp.concatenate([reached] * 4, axis=0) > 0.5
    tree_score = lax.dot_general(q, t_s[:, 0:HD], dims, preferred_element_type=F32) * scaling
    tree_score = jnp.where(tree_mask, tree_score, NEG)
    peak = jnp.max(tree_score, axis=1, keepdims=True)
    scores = []
    for p in range(4):
        key = got[0:32, p].reshape(256, HD)
        score = lax.dot_general(q, key, dims, preferred_element_type=F32) * scaling
        seen = iota((4 * TOK, 256), 1) < length - p * 256
        score = jnp.where(seen, score, NEG)
        peak = jnp.maximum(peak, jnp.max(score, axis=1, keepdims=True))
        scores.append(score)
    expo = jnp.where(tree_mask, jnp.exp(tree_score - peak), 0.0)
    denom = jnp.sum(expo, axis=1, keepdims=True)
    numer = jnp.dot(expo.astype(BF16), t_s[:, HD : 2 * HD], preferred_element_type=F32)
    for p in range(4):
        seen = iota((4 * TOK, 256), 1) < length - p * 256
        expo = jnp.where(seen, jnp.exp(scores[p] - peak), 0.0)
        denom = denom + jnp.sum(expo, axis=1, keepdims=True)
        value = got[32:64, p].reshape(256, HD)
        numer = numer + jnp.dot(expo.astype(BF16), value, preferred_element_type=F32)
    attention = (numer / denom).astype(BF16)
    for m in range(8):
        out[m] = attention


def append_body(owner, lens, path, cache, aux, out):
    slots = cache.shape[0]
    depth = path.shape[1]
    for s in range(slots):
        r = jnp.maximum(owner[s, 0], 0)
        count = jnp.int32(0)
        for d in range(depth):
            count = count + jnp.where(path[r, d] >= 0, 1, 0)
        count = jnp.where(owner[s, 0] >= 0, count, 0)
        first = lens[r] - owner[s, 1] * 256
        key = jnp.concatenate([aux[4 * s, 0, 4:8], aux[4 * s + 1, 0, 4:8]], axis=0)
        value = jnp.concatenate([aux[4 * s + 2, 0, 4:8], aux[4 * s + 3, 0, 4:8]], axis=0)
        fresh = jnp.concatenate([key, value], axis=1)
        pick = (iota((256, depth), 0) - first == iota((256, depth), 1)).astype(BF16)
        put = jnp.dot(pick, fresh, preferred_element_type=F32).astype(BF16)
        offset = iota((256, 2 * HD), 0) - first
        out[s] = jnp.where((offset >= 0) & (offset < count), put, cache[s])


def project_body(att, weight, out):
    left = jnp.concatenate([att[:, 0:TOK].reshape(256, HD), att[:, TOK : 2 * TOK].reshape(256, HD)], axis=1)
    right = jnp.concatenate(
        [att[:, 2 * TOK : 3 * TOK].reshape(256, HD), att[:, 3 * TOK : 4 * TOK].reshape(256, HD)], axis=1
    )
    low = iota((HD, HD), 1) < 64
    for c in range(8):
        x = jnp.dot(left, weight[c], preferred_element_type=F32)
        y = jnp.dot(right, weight[c], preferred_element_type=F32)
        first = x[0:128] + pltpu.roll(y[0:128], 64, 1)
        second = pltpu.roll(x[128:256], 64, 1) + y[128:256]
        out[c] = jnp.where(low, first, second).astype(BF16)


def total_body(got, out):
    acc = got[0].astype(F32)
    for k in range(1, 8):
        acc = acc + got[k].astype(F32)
    out[...] = acc.astype(BF16)


def place_body(got, out):
    tokens = out.shape[1]
    for h in range(2):
        for b in range(4):
            out[4 * h + b] = got[b * TOK : b * TOK + tokens, 64 * h : 64 * h + 64]


VM = pl.BlockSpec(memory_space=pltpu.VMEM)
SM = pl.BlockSpec(memory_space=pltpu.SMEM)


def call(body, name, specs, shape, scratch=()):
    return pl.pallas_call(
        body,
        name=name,
        in_specs=list(specs),
        out_specs=VM,
        out_shape=jax.ShapeDtypeStruct(shape, BF16),
        scratch_shapes=list(scratch),
    )


def shards(queries, tree_kv, tree_parent, accepted_path, cache_kv, piece_owner, cache_len, out_weight):
    tokens = queries.shape[1]
    to_all = functools.partial(lax.all_to_all, split_axis=0, concat_axis=0, tiled=True)
    near = [[8 * a + b for b in range(8)] for a in range(8)]
    far = [[8 * a + b for a in range(8)] for b in range(8)]
    with jax.named_scope("weight_gather"):
        half = out_weight.shape[0] // 2
        wide = jnp.concatenate([out_weight[:half], out_weight[half:]], axis=1)
        weight = to_all(jnp.broadcast_to(wide[None], (8,) + wide.shape), "req", axis_index_groups=far)
    with jax.named_scope("spread"):
        packed = call(pack_body, "pack", (SM, SM, VM, VM), (64, 4, 8, HD))(
            piece_owner, accepted_path, cache_kv, tree_kv
        )
        pieces = to_all(packed, "req")
    with jax.named_scope("route"):
        routed = call(
            route_body,
            "route",
            (VM,),
            (64, 5, 8, HD),
            [pltpu.VMEM((2, 256), jnp.int32), pltpu.SMEM((2, 256), jnp.int32), pltpu.SemaphoreType.DMA],
        )(pieces)
        home = to_all(routed, "req")
    with jax.named_scope("attend"):
        attention = call(
            attend_body,
            "attend",
            (SM, VM, VM, VM, VM),
            (8, 4 * TOK, HD),
            [pltpu.VMEM((4 * TOK, HD), BF16), pltpu.VMEM((TOK, 2 * HD), BF16)],
        )(cache_len, queries, tree_kv, tree_parent, home)
        gathered = to_all(attention, "req", axis_index_groups=near)
    with jax.named_scope("append"):
        cache_out = call(append_body, "append", (SM, SM, SM, VM, VM), cache_kv.shape)(
            piece_owner, cache_len, accepted_path, cache_kv, home[:12, 4:5]
        )
    with jax.named_scope("project"):
        partial = call(project_body, "project", (VM, VM), (8, 128, HD))(gathered, weight)
        partials = to_all(partial, "tp")
        total = call(total_body, "total", (VM,), (128, HD))(partials)
        pairs = [((8 * a + b) * 8 + c, (8 * c + b) * 8 + a) for a in range(8) for b in range(8) for c in range(8)]
        final = lax.ppermute(total, ("req", "tp"), pairs)
        mixed = call(place_body, "place", (VM,), (8, tokens, 64))(final)
    return (mixed, cache_out)


def solution(mesh):
    return jax.shard_map(
        shards,
        mesh=mesh,
        in_specs=(
            P("req", None, "tp"),
            P("req", None, "tp"),
            P("req", None),
            P(),
            P("req", None, "tp"),
            P("req", None),
            P(),
            P("tp", "req"),
        ),
        out_specs=(P("tp", None, "req"), P("req", None, "tp")),
        check_vma=False,
    )
```

```python
import functools
import math

import jax
import jax.numpy as jnp
from jax import lax
from jax.experimental import pallas as pl
from jax.experimental.pallas import tpu as pltpu
from jax.sharding import PartitionSpec as P

HD = 128
NEG = -1e30
TOKENS = 28
TOK = 32
QUERY_AT = 12
TREE_AT = 28
PARENT_AT = 36
F32 = jnp.float32
BF16 = jnp.bfloat16


def iota(shape, dim):
    return lax.broadcasted_iota(jnp.int32, shape, dim)


def pack_body(owner, path, cache, query, tree, parent, out, query_f, tree_f, aux):
    slots = cache.shape[0]
    tokens = tree.shape[1]
    depth = path.shape[0]
    own = lax.axis_index("req")
    for s in range(slots):
        out[0:32, s] = cache[s, :, 0:HD].reshape(32, 8, HD)
        out[32:64, s] = cache[s, :, HD : 2 * HD].reshape(32, 8, HD)
    query_f[...] = query[0].astype(F32)
    tree_f[...] = tree[0].astype(F32)
    keys = jnp.full((8, HD), -1, jnp.int32)
    for s in range(slots):
        key = jnp.where(owner[0, s] >= 0, owner[0, s] * 4 + owner[1, s], -1)
        keys = jnp.where(iota((8, HD), 1) == s, key, keys)
    keyrow = jnp.where(iota((8, HD), 0) == 0, keys, 0).astype(F32)
    aux[...] = jnp.broadcast_to(keyrow[None], (64, 8, HD))
    hot_col = iota((depth, tokens), 1)
    hot_row = iota((depth, tokens), 0)
    hot = jnp.zeros((depth, tokens), jnp.bool_)
    for d in range(depth):
        hot = hot | ((hot_row == d) & (hot_col == path[d, own]))
    rows = jnp.dot(hot.astype(BF16), tree[0], preferred_element_type=F32)
    for h in range(4):
        chunk = rows[4 * (h % 2) : 4 * (h % 2) + 4, HD * (h // 2) : HD * (h // 2) + HD]
        for i in range(slots):
            aux[4 * i + h, 4:8] = chunk
    for g in range(4):
        for m in range(4):
            aux[QUERY_AT + 4 * g + m, 1:8] = query_f[7 * m : 7 * m + 7, g * HD : (g + 1) * HD]
    for g in range(2):
        for m in range(4):
            aux[TREE_AT + 4 * g + m, 1:8] = tree_f[7 * m : 7 * m + 7, g * HD : (g + 1) * HD]
    aux[PARENT_AT, 1:2, 0:tokens] = parent[...].astype(F32)
    out[:, 3] = aux[...].astype(BF16)


def route_body(got, out, table, table_s, sem):
    own = lax.axis_index("req")
    which = jnp.minimum(own // 4, 2)
    keys = got[:, 3, 0:1, :].astype(F32).reshape(64, HD)
    source = iota((64, 256), 0)
    lane = iota((64, 256), 1)
    place = lane // 4
    asked = place_request(place) * 4 + lane % 4
    target = asked.astype(F32)
    found = jnp.zeros((64, 256), F32)
    mine = jnp.zeros((64, 1), F32)
    tile = (source * 4).astype(F32)
    for i in range(3):
        key = keys[:, i : i + 1]
        found = found + jnp.where(key == target, tile + float(i), 0.0)
        mine = jnp.where(which == i, key, mine)
    holder = jnp.floor(jnp.maximum(mine, 0.0) * 0.25)
    holder = jnp.sum(jnp.where(source == lane, holder, 0.0), axis=0, keepdims=True)
    home = place_request(lane[0:1]).astype(F32)
    rows = jnp.where(own < QUERY_AT, holder, home) * 4.0 + 3.0
    found = jnp.sum(found, axis=0, keepdims=True)
    table[...] = jnp.concatenate([found, rows], axis=0).astype(jnp.int32)
    copy = pltpu.make_async_copy(table, table_s, sem)
    copy.start()
    copy.wait()

    def step(r, carry):
        for p in range(4):
            t = table_s[0, 4 * r + p]
            out[r, p] = got[t >> 2, t & 3]
        out[r, 4] = got[table_s[1, r] >> 2, 3]
        return carry

    lax.fori_loop(0, 64, step, 0, unroll=8)


def place_request(place):
    return (place // 16) * 16 + (place % 2) * 8 + (place // 2) % 8


def closure(parent):
    n = TOK
    up = iota((n, n), 0).astype(F32)
    here = iota((n, n), 1).astype(F32)
    eye = (up == here).astype(F32)
    reach = jnp.minimum((up == parent).astype(F32) + eye, 1.0)
    for rounds in range(5):
        low = reach.astype(BF16)
        reach = jnp.minimum(jnp.dot(low, low, preferred_element_type=F32), 1.0)
    return lax.dot_general(
        reach.astype(BF16), eye.astype(BF16), (((0,), (0,)), ((), ())), preferred_element_type=F32
    )


def attend_body(lens, got, out, query_f, tree_f):
    length = lens[place_request(lax.axis_index("req"))]
    query_f[...] = jnp.zeros_like(query_f)
    tree_f[...] = jnp.zeros_like(tree_f)
    for g in range(4):
        for m in range(4):
            at = g * TOK + 7 * m
            query_f[at : at + 7] = got[QUERY_AT + 4 * g + m, 4].astype(F32)[1:8]
    for g in range(2):
        for m in range(4):
            tree_f[7 * m : 7 * m + 7, g * HD : (g + 1) * HD] = got[TREE_AT + 4 * g + m, 4].astype(F32)[1:8]
    parent = got[PARENT_AT, 4].astype(F32)[1:2, 0:TOK]
    q = query_f[...].astype(BF16)
    fresh = tree_f[...].astype(BF16)
    scaling = 1.0 / math.sqrt(HD)
    dims = (((1,), (1,)), ((), ()))
    reached = closure(parent)
    tree_mask = jnp.concatenate([reached] * 4, axis=0) > 0.5
    tree_score = lax.dot_general(q, fresh[:, 0:HD], dims, preferred_element_type=F32) * scaling
    tree_score = jnp.where(tree_mask, tree_score, NEG)
    peak = jnp.max(tree_score, axis=1, keepdims=True)
    scores = []
    for p in range(4):
        key = got[0:32, p].reshape(256, HD)
        score = lax.dot_general(q, key, dims, preferred_element_type=F32) * scaling
        seen = iota((4 * TOK, 256), 1) < length - p * 256
        score = jnp.where(seen, score, NEG)
        peak = jnp.maximum(peak, jnp.max(score, axis=1, keepdims=True))
        scores.append(score)
    expo = jnp.where(tree_mask, jnp.exp(tree_score - peak), 0.0)
    denom = jnp.sum(expo, axis=1, keepdims=True)
    numer = jnp.dot(expo.astype(BF16), fresh[:, HD : 2 * HD], preferred_element_type=F32)
    for p in range(4):
        seen = iota((4 * TOK, 256), 1) < length - p * 256
        expo = jnp.where(seen, jnp.exp(scores[p] - peak), 0.0)
        denom = denom + jnp.sum(expo, axis=1, keepdims=True)
        value = got[32:64, p].reshape(256, HD)
        numer = numer + jnp.dot(expo.astype(BF16), value, preferred_element_type=F32)
    attention = (numer / denom).astype(BF16)
    for m in range(8):
        out[m] = attention


def append_body(owner, lens, path, cache, got, out):
    slots = cache.shape[0]
    depth = path.shape[0]
    for s in range(slots):
        r = jnp.maximum(owner[0, s], 0)
        count = jnp.int32(0)
        for d in range(depth):
            count = count + jnp.where(path[d, r] >= 0, 1, 0)
        count = jnp.where(owner[0, s] >= 0, count, 0)
        first = lens[r] - owner[1, s] * 256
        key = jnp.concatenate([got[4 * s, 4, 4:8], got[4 * s + 1, 4, 4:8]], axis=0)
        value = jnp.concatenate([got[4 * s + 2, 4, 4:8], got[4 * s + 3, 4, 4:8]], axis=0)
        fresh = jnp.concatenate([key, value], axis=1)
        pick = (iota((256, depth), 0) - first == iota((256, depth), 1)).astype(BF16)
        put = jnp.dot(pick, fresh, preferred_element_type=F32).astype(BF16)
        offset = iota((256, 2 * HD), 0) - first
        out[s] = jnp.where((offset >= 0) & (offset < count), put, cache[s])


def project_body(att, weight, out):
    rows = 8 * TOKENS
    pick = iota((rows, 256), 1) == (iota((rows, 256), 0) % 8) * TOK + iota((rows, 256), 0) // 8
    pick = pick.astype(BF16)
    parts = [att[:, g * TOK : (g + 1) * TOK].reshape(256, HD) for g in range(4)]
    both = jnp.dot(pick, jnp.concatenate(parts, axis=1), preferred_element_type=F32).astype(BF16)
    product = lax.dot_general(
        both, weight[...].reshape(512, 512), (((1,), (1,)), ((), ())), preferred_element_type=F32
    )
    half = rows // 2
    low = iota((half, HD), 1) < 64
    for c in range(8):
        x = product[:, HD * (c // 2) : HD * (c // 2) + HD]
        if c % 2 == 0:
            block = jnp.where(low, x[0:half], pltpu.roll(x[half:rows], 64, 1))
        else:
            block = jnp.where(low, pltpu.roll(x[0:half], 64, 1), x[half:rows])
        out[c] = block.astype(BF16)


def total_body(got, out):
    acc = got[0].astype(F32)
    for k in range(1, 8):
        acc = acc + got[k].astype(F32)
    out[...] = acc.astype(BF16)


def place_body(got, out):
    half = TOKENS // 2
    out[0:half] = got[:, 0:64].reshape(half, 8, 64)
    out[half:TOKENS] = got[:, 64:128].reshape(half, 8, 64)


VM = pl.BlockSpec(memory_space=pltpu.VMEM)
SM = pl.BlockSpec(memory_space=pltpu.SMEM)


def near(x):
    return pltpu.with_memory_space_constraint(x, pltpu.VMEM)


def call(body, name, specs, out, scratch=()):
    return pl.pallas_call(
        body, name=name, in_specs=list(specs), out_specs=VM, out_shape=out, scratch_shapes=list(scratch)
    )


def shards(queries, tree_kv, tree_parent, accepted_path, cache_kv, piece_owner, cache_len, out_weight):
    tokens = queries.shape[1]
    to_all = functools.partial(lax.all_to_all, split_axis=0, concat_axis=0, tiled=True)
    spot = [[16 * (a // 2) + 2 * b + a % 2 for b in range(8)] for a in range(8)]
    same_group = spot
    same_row = [[spot[a][b] for a in range(8)] for b in range(8)]
    owner = piece_owner.T
    path = accepted_path.T
    with jax.named_scope("weight_gather"):
        columns = out_weight.T
        weight = to_all(jnp.broadcast_to(columns[None], (8,) + columns.shape), "req", axis_index_groups=same_row)
    with jax.named_scope("spread"):
        packed = call(
            pack_body,
            "pack",
            (SM, SM, VM, VM, VM, VM),
            pltpu.VMEM((64, 4, 8, HD), BF16),
            [pltpu.VMEM((tokens, 4 * HD), F32), pltpu.VMEM((tokens, 2 * HD), F32), pltpu.VMEM((64, 8, HD), F32)],
        )(owner, path, cache_kv, queries, tree_kv, tree_parent)
        packed, weight = lax.optimization_barrier((packed, weight))
        pieces = to_all(packed, "req")
    with jax.named_scope("route"):
        routed = call(
            route_body,
            "route",
            (VM,),
            pltpu.VMEM((64, 5, 8, HD), BF16),
            [pltpu.VMEM((2, 256), jnp.int32), pltpu.SMEM((2, 256), jnp.int32), pltpu.SemaphoreType.DMA],
        )(near(pieces))
        home = near(to_all(routed, "req"))
    with jax.named_scope("attend"):
        attention = call(
            attend_body,
            "attend",
            (SM, VM),
            pltpu.VMEM((8, 4 * TOK, HD), BF16),
            [pltpu.VMEM((4 * TOK, HD), F32), pltpu.VMEM((TOK, 2 * HD), F32)],
        )(cache_len, home)
        gathered = to_all(attention, "req", axis_index_groups=same_group)
    with jax.named_scope("append"):
        cache_out = call(
            append_body, "append", (SM, SM, SM, VM, VM), jax.ShapeDtypeStruct(cache_kv.shape, BF16)
        )(owner, cache_len, path, cache_kv, home)
    with jax.named_scope("project"):
        partial = call(project_body, "project", (VM, VM), pltpu.VMEM((8, 4 * TOKENS, HD), BF16))(
            near(gathered), near(weight)
        )
        partials = to_all(partial, "tp")
        total = call(total_body, "total", (VM,), pltpu.VMEM((4 * TOKENS, HD), BF16))(near(partials))
        pairs = [(spot[a][b] * 8 + c, spot[c][b] * 8 + a) for a in range(8) for b in range(8) for c in range(8)]
        final = lax.ppermute(total, ("req", "tp"), pairs)
        mixed = call(place_body, "place", (VM,), jax.ShapeDtypeStruct((TOKENS, 8, 64), BF16))(near(final))
    return (mixed.transpose(1, 0, 2), cache_out)


def solution(mesh):
    return jax.shard_map(
        shards,
        mesh=mesh,
        in_specs=(
            P("req", None, "tp"),
            P("req", None, "tp"),
            P("req", None),
            P(),
            P("req", None, "tp"),
            P("req", None),
            P(),
            P("tp", "req"),
        ),
        out_specs=(P("tp", None, "req"), P("req", None, "tp")),
        check_vma=False,
    )
```

```python
import functools
import math

import jax
import jax.numpy as jnp
from jax import lax
from jax.experimental import pallas as pl
from jax.experimental.pallas import tpu as pltpu
from jax.sharding import PartitionSpec as P

HD = 128
NEG = -1e30
TOKENS = 28
TOK = 32
QUERY_AT = 12
TREE_AT = 28
PARENT_AT = 36
ORDER = (0, 4, 1, 5, 3, 7, 2, 6)
F32 = jnp.float32
BF16 = jnp.bfloat16


def iota(shape, dim):
    return lax.broadcasted_iota(jnp.int32, shape, dim)


def pack_body(owner, path, cache, query, tree, parent, out, query_f, tree_f, aux):
    slots = cache.shape[0]
    tokens = tree.shape[1]
    depth = path.shape[0]
    own = lax.axis_index("req")
    for s in range(slots):
        out[0:32, s] = cache[s, :, 0:HD].reshape(32, 8, HD)
        out[32:64, s] = cache[s, :, HD : 2 * HD].reshape(32, 8, HD)
    query_f[...] = query[0].astype(F32)
    tree_f[...] = tree[0].astype(F32)
    keys = jnp.full((8, HD), -1, jnp.int32)
    for s in range(slots):
        key = jnp.where(owner[0, s] >= 0, owner[0, s] * 4 + owner[1, s], -1)
        keys = jnp.where(iota((8, HD), 1) == s, key, keys)
    keyrow = jnp.where(iota((8, HD), 0) == 0, keys, 0).astype(F32)
    aux[...] = jnp.broadcast_to(keyrow[None], (64, 8, HD))
    hot_col = iota((depth, tokens), 1)
    hot_row = iota((depth, tokens), 0)
    hot = jnp.zeros((depth, tokens), jnp.bool_)
    for d in range(depth):
        hot = hot | ((hot_row == d) & (hot_col == path[d, own]))
    rows = jnp.dot(hot.astype(BF16), tree[0], preferred_element_type=F32)
    for h in range(4):
        chunk = rows[4 * (h % 2) : 4 * (h % 2) + 4, HD * (h // 2) : HD * (h // 2) + HD]
        for i in range(slots):
            aux[4 * i + h, 4:8] = chunk
    for g in range(4):
        for m in range(4):
            aux[QUERY_AT + 4 * g + m, 1:8] = query_f[7 * m : 7 * m + 7, g * HD : (g + 1) * HD]
    for g in range(2):
        for m in range(4):
            aux[TREE_AT + 4 * g + m, 1:8] = tree_f[7 * m : 7 * m + 7, g * HD : (g + 1) * HD]
    aux[PARENT_AT, 1:2, 0:tokens] = parent[...].astype(F32)
    out[:, 3] = aux[...].astype(BF16)


def route_body(got, out, table, table_s, sem):
    own = lax.axis_index("req")
    which = jnp.minimum(own // 4, 2)
    keys = got[:, 3, 0:1, :].astype(F32).reshape(64, HD)
    source = iota((64, 256), 0)
    lane = iota((64, 256), 1)
    place = lane // 4
    asked = place_request(place) * 4 + lane % 4
    target = asked.astype(F32)
    found = jnp.zeros((64, 256), F32)
    mine = jnp.zeros((64, 1), F32)
    tile = (source * 4).astype(F32)
    for i in range(3):
        key = keys[:, i : i + 1]
        found = found + jnp.where(key == target, tile + float(i), 0.0)
        mine = jnp.where(which == i, key, mine)
    holder = jnp.floor(jnp.maximum(mine, 0.0) * 0.25)
    holder = jnp.sum(jnp.where(source == lane, holder, 0.0), axis=0, keepdims=True)
    home = place_request(lane[0:1]).astype(F32)
    rows = jnp.where(own < QUERY_AT, holder, home) * 4.0 + 3.0
    found = jnp.sum(found, axis=0, keepdims=True)
    table[...] = jnp.concatenate([found, rows], axis=0).astype(jnp.int32)
    copy = pltpu.make_async_copy(table, table_s, sem)
    copy.start()
    copy.wait()

    def step(r, carry):
        for p in range(4):
            t = table_s[0, 4 * r + p]
            out[r, p] = got[t >> 2, t & 3]
        out[r, 4] = got[table_s[1, r] >> 2, 3]
        return carry

    lax.fori_loop(0, 64, step, 0, unroll=8)


def place_request(place):
    return (place % 2) * 32 + (place // 16) * 8 + (place // 2) % 8


def closure(parent):
    n = TOK
    up = iota((n, n), 0).astype(F32)
    here = iota((n, n), 1).astype(F32)
    eye = (up == here).astype(F32)
    reach = jnp.minimum((up == parent).astype(F32) + eye, 1.0)
    for rounds in range(5):
        low = reach.astype(BF16)
        reach = jnp.minimum(jnp.dot(low, low, preferred_element_type=F32), 1.0)
    return lax.dot_general(
        reach.astype(BF16), eye.astype(BF16), (((0,), (0,)), ((), ())), preferred_element_type=F32
    )


def attend_body(lens, got, out, query_f, tree_f):
    length = lens[place_request(lax.axis_index("req"))]
    query_f[...] = jnp.zeros_like(query_f)
    tree_f[...] = jnp.zeros_like(tree_f)
    for g in range(4):
        for m in range(4):
            at = g * TOK + 7 * m
            query_f[at : at + 7] = got[QUERY_AT + 4 * g + m, 4].astype(F32)[1:8]
    for g in range(2):
        for m in range(4):
            tree_f[7 * m : 7 * m + 7, g * HD : (g + 1) * HD] = got[TREE_AT + 4 * g + m, 4].astype(F32)[1:8]
    parent = got[PARENT_AT, 4].astype(F32)[1:2, 0:TOK]
    q = query_f[...].astype(BF16)
    fresh = tree_f[...].astype(BF16)
    scaling = 1.0 / math.sqrt(HD)
    dims = (((1,), (1,)), ((), ()))
    reached = closure(parent)
    tree_mask = jnp.concatenate([reached] * 4, axis=0) > 0.5
    tree_score = lax.dot_general(q, fresh[:, 0:HD], dims, preferred_element_type=F32) * scaling
    tree_score = jnp.where(tree_mask, tree_score, NEG)
    peak = jnp.max(tree_score, axis=1, keepdims=True)
    scores = []
    for p in range(4):
        key = got[0:32, p].reshape(256, HD)
        score = lax.dot_general(q, key, dims, preferred_element_type=F32) * scaling
        seen = iota((4 * TOK, 256), 1) < length - p * 256
        score = jnp.where(seen, score, NEG)
        peak = jnp.maximum(peak, jnp.max(score, axis=1, keepdims=True))
        scores.append(score)
    expo = jnp.where(tree_mask, jnp.exp(tree_score - peak), 0.0)
    denom = jnp.sum(expo, axis=1, keepdims=True)
    numer = jnp.dot(expo.astype(BF16), fresh[:, HD : 2 * HD], preferred_element_type=F32)
    for p in range(4):
        seen = iota((4 * TOK, 256), 1) < length - p * 256
        expo = jnp.where(seen, jnp.exp(scores[p] - peak), 0.0)
        denom = denom + jnp.sum(expo, axis=1, keepdims=True)
        value = got[32:64, p].reshape(256, HD)
        numer = numer + jnp.dot(expo.astype(BF16), value, preferred_element_type=F32)
    attention = (numer / denom).astype(BF16)
    for m in range(8):
        out[m] = attention


def append_body(owner, lens, path, cache, got, out):
    slots = cache.shape[0]
    depth = path.shape[0]
    for s in range(slots):
        r = jnp.maximum(owner[0, s], 0)
        count = jnp.int32(0)
        for d in range(depth):
            count = count + jnp.where(path[d, r] >= 0, 1, 0)
        count = jnp.where(owner[0, s] >= 0, count, 0)
        first = lens[r] - owner[1, s] * 256
        key = jnp.concatenate([got[4 * s, 4, 4:8], got[4 * s + 1, 4, 4:8]], axis=0)
        value = jnp.concatenate([got[4 * s + 2, 4, 4:8], got[4 * s + 3, 4, 4:8]], axis=0)
        fresh = jnp.concatenate([key, value], axis=1)
        pick = (iota((256, depth), 0) - first == iota((256, depth), 1)).astype(BF16)
        put = jnp.dot(pick, fresh, preferred_element_type=F32).astype(BF16)
        offset = iota((256, 2 * HD), 0) - first
        out[s] = jnp.where((offset >= 0) & (offset < count), put, cache[s])


def project_body(att, first_weight, last_weight, out):
    rows = 8 * TOKENS
    pick = iota((rows, 256), 1) == (iota((rows, 256), 0) % 8) * TOK + iota((rows, 256), 0) // 8
    pick = pick.astype(BF16)
    parts = [att[:, g * TOK : (g + 1) * TOK].reshape(256, HD) for g in range(4)]
    both = jnp.dot(pick, jnp.concatenate(parts, axis=1), preferred_element_type=F32).astype(BF16)
    own = lax.axis_index("req")
    mine = (own % 2) * 4 + own // 16
    half = rows // 2
    low = iota((half, HD), 1) < 64
    dims = (((1,), (1,)), ((), ()))
    for part, weight in enumerate((first_weight, last_weight)):
        product = lax.dot_general(both, weight[...].reshape(256, 512), dims, preferred_element_type=F32)
        for i in range(4):
            x = product[:, HD * (i // 2) : HD * (i // 2) + HD]
            if i % 2 == 0:
                block = jnp.where(low, x[0:half], pltpu.roll(x[half:rows], 64, 1))
            else:
                block = jnp.where(low, pltpu.roll(x[0:half], 64, 1), x[half:rows])
            out[mine ^ ORDER[4 * part + i]] = block.astype(BF16)


def total_body(got, out):
    acc = got[0].astype(F32)
    for k in range(1, 8):
        acc = acc + got[k].astype(F32)
    out[...] = acc.astype(BF16)


def place_body(got, out):
    half = TOKENS // 2
    out[0:half] = got[:, 0:64].reshape(half, 8, 64)
    out[half:TOKENS] = got[:, 64:128].reshape(half, 8, 64)


VM = pl.BlockSpec(memory_space=pltpu.VMEM)
SM = pl.BlockSpec(memory_space=pltpu.SMEM)


def near(x):
    return pltpu.with_memory_space_constraint(x, pltpu.VMEM)


def call(body, name, specs, out, scratch=()):
    return pl.pallas_call(
        body, name=name, in_specs=list(specs), out_specs=VM, out_shape=out, scratch_shapes=list(scratch)
    )


def shards(queries, tree_kv, tree_parent, accepted_path, cache_kv, piece_owner, cache_len, out_weight):
    tokens = queries.shape[1]
    to_all = functools.partial(lax.all_to_all, split_axis=0, concat_axis=0, tiled=True)
    spot = [[16 * (a % 4) + 2 * b + a // 4 for b in range(8)] for a in range(8)]

    def swap(x, flip):
        return lax.ppermute(x, "req", [(spot[a][b], spot[a ^ flip][b]) for a in range(8) for b in range(8)])

    owner = piece_owner.T
    path = accepted_path.T
    with jax.named_scope("weight_gather"):
        one = out_weight.T[None]
        other = swap(one, 4)
    with jax.named_scope("spread"):
        packed = call(
            pack_body,
            "pack",
            (SM, SM, VM, VM, VM, VM),
            pltpu.VMEM((64, 4, 8, HD), BF16),
            [pltpu.VMEM((tokens, 4 * HD), F32), pltpu.VMEM((tokens, 2 * HD), F32), pltpu.VMEM((64, 8, HD), F32)],
        )(owner, path, cache_kv, queries, tree_kv, tree_parent)
        pieces = to_all(packed, "req")
        pieces, other = lax.optimization_barrier((pieces, other))
    with jax.named_scope("weight_gather"):
        pair = jnp.concatenate([one, other])
        other_pair = swap(pair, 1)
    with jax.named_scope("route"):
        routed = call(
            route_body,
            "route",
            (VM,),
            pltpu.VMEM((64, 5, 8, HD), BF16),
            [pltpu.VMEM((2, 256), jnp.int32), pltpu.SMEM((2, 256), jnp.int32), pltpu.SemaphoreType.DMA],
        )(near(pieces))
        home = to_all(routed, "req")
        home, other_pair = lax.optimization_barrier((home, other_pair))
        home = near(home)
    with jax.named_scope("weight_gather"):
        first_weight = jnp.concatenate([pair, other_pair])
        last_weight = swap(first_weight, 3)
    with jax.named_scope("attend"):
        attention = call(
            attend_body,
            "attend",
            (SM, VM),
            pltpu.VMEM((8, 4 * TOK, HD), BF16),
            [pltpu.VMEM((4 * TOK, HD), F32), pltpu.VMEM((TOK, 2 * HD), F32)],
        )(cache_len, home)
        gathered = to_all(attention, "req", axis_index_groups=spot)
        gathered, last_weight = lax.optimization_barrier((gathered, last_weight))
    with jax.named_scope("append"):
        cache_out = call(
            append_body, "append", (SM, SM, SM, VM, VM), jax.ShapeDtypeStruct(cache_kv.shape, BF16)
        )(owner, cache_len, path, cache_kv, home)
    with jax.named_scope("project"):
        partial = call(project_body, "project", (VM, VM, VM), pltpu.VMEM((8, 4 * TOKENS, HD), BF16))(
            near(gathered), near(first_weight), near(last_weight)
        )
        partials = to_all(partial, "tp")
        total = call(total_body, "total", (VM,), pltpu.VMEM((4 * TOKENS, HD), BF16))(near(partials))
        pairs = [(spot[a][b] * 8 + c, spot[c][b] * 8 + a) for a in range(8) for b in range(8) for c in range(8)]
        final = lax.ppermute(total, ("req", "tp"), pairs)
        mixed = call(place_body, "place", (VM,), jax.ShapeDtypeStruct((TOKENS, 8, 64), BF16))(near(final))
    return (mixed.transpose(1, 0, 2), cache_out)


def solution(mesh):
    return jax.shard_map(
        shards,
        mesh=mesh,
        in_specs=(
            P("req", None, "tp"),
            P("req", None, "tp"),
            P("req", None),
            P(),
            P("req", None, "tp"),
            P("req", None),
            P(),
            P("tp", "req"),
        ),
        out_specs=(P("tp", None, "req"), P("req", None, "tp")),
        check_vma=False,
    )
```

```python
import functools
import math

import jax
import jax.numpy as jnp
from jax import lax
from jax.experimental import pallas as pl
from jax.experimental.pallas import tpu as pltpu
from jax.sharding import PartitionSpec as P

HD = 128
NEG = -1e30
TOKENS = 28
TOK = 32
ORDER = (0, 1, 4, 5, 3, 2, 7, 6)
F32 = jnp.float32
BF16 = jnp.bfloat16


def iota(shape, dim):
    return lax.broadcasted_iota(jnp.int32, shape, dim)


def pack_body(owner, path, cache, query, tree, parent, out, rows, aux):
    slots = cache.shape[0]
    tokens = tree.shape[1]
    depth = path.shape[0]
    own = lax.axis_index("req")
    for s in range(slots):
        out[0:32, s] = cache[s, :, 0:HD].reshape(32, 8, HD)
        out[32:64, s] = cache[s, :, HD : 2 * HD].reshape(32, 8, HD)
    keys = jnp.full((8, HD), -1, jnp.int32)
    for s in range(slots):
        key = jnp.where(owner[0, s] >= 0, owner[0, s] * 4 + owner[1, s], -1)
        keys = jnp.where(iota((8, HD), 1) == s, key, keys)
    keyrow = jnp.where(iota((8, HD), 0) == 0, keys, 0).astype(F32)
    hot_col = iota((depth, tokens), 1)
    hot_row = iota((depth, tokens), 0)
    hot = jnp.zeros((depth, tokens), jnp.bool_)
    for d in range(depth):
        hot = hot | ((hot_row == d) & (hot_col == path[d, own]))
    fresh = jnp.dot(hot.astype(BF16), tree[0], preferred_element_type=F32)
    for y in range(8):
        aux[...] = keyrow
        two = fresh[2 * (y % 4) : 2 * (y % 4) + 2, HD * (y // 4) : HD * (y // 4) + HD]
        for i in range(slots):
            aux[2 + 2 * i : 4 + 2 * i] = two
        tile = aux[...].astype(BF16)
        for x in range(4):
            for core in range(2):
                out[16 * x + 2 * y + core, 3] = tile
    rows[...] = jnp.zeros_like(rows)
    rows[0:tokens, 0 : 4 * HD] = query[0]
    rows[0:tokens, 4 * HD : 6 * HD] = tree[0]
    rows[tokens : tokens + 1, 0:tokens] = parent[...].astype(F32).astype(BF16)


def route_body(got, out, fresh, table, table_s, sem):
    own = lax.axis_index("req")
    keys = got[:, 3, 0:1, :].astype(F32).reshape(64, HD)
    source = iota((64, 256), 0)
    lane = iota((64, 256), 1)
    target = (place_request(lane // 4) * 4 + lane % 4).astype(F32)
    tile = (source * 4).astype(F32)
    diagonal = source == lane
    found = jnp.zeros((64, 256), F32)
    holders = []
    for i in range(3):
        key = keys[:, i : i + 1]
        found = found + jnp.where(key == target, tile + float(i), 0.0)
        request = jnp.floor(jnp.maximum(key, 0.0) * 0.25)
        holders.append(jnp.sum(jnp.where(diagonal, request, 0.0), axis=0, keepdims=True))
    found = jnp.minimum(jnp.sum(found, axis=0, keepdims=True), 255.0)
    table[...] = jnp.concatenate([found] + holders, axis=0).astype(jnp.int32)
    copy = pltpu.make_async_copy(table, table_s, sem)
    copy.start()
    copy.wait()

    def step(r, carry):
        for p in range(4):
            t = table_s[0, 4 * r + p]
            out[r, p] = got[t >> 2, t & 3]
        return carry

    lax.fori_loop(0, 64, step, 0, unroll=8)
    row = iota((8, HD), 0)
    for y in range(8):
        holder = (own // 16) * 16 + 2 * y + own % 2
        tiles = [got[table_s[1 + i, holder], 3].astype(F32) for i in range(3)]
        fresh[y] = jnp.where(row < 4, tiles[0], jnp.where(row < 6, tiles[1], tiles[2])).astype(BF16)


def place_request(place):
    group = (place % 2) * 4 + place // 16
    return group * 8 + (place // 2 + 4 * (group % 2) + 2) % 8


def closure(parent):
    n = TOK
    up = iota((n, n), 0).astype(F32)
    here = iota((n, n), 1).astype(F32)
    eye = (up == here).astype(F32)
    reach = jnp.minimum((up == parent).astype(F32) + eye, 1.0)
    for rounds in range(5):
        low = reach.astype(BF16)
        reach = jnp.minimum(jnp.dot(low, low, preferred_element_type=F32), 1.0)
    return lax.dot_general(
        reach.astype(BF16), eye.astype(BF16), (((0,), (0,)), ((), ())), preferred_element_type=F32
    )


def attend_body(lens, own_rows, got, fresh_rows, out):
    length = lens[place_request(lax.axis_index("req"))]
    q = jnp.concatenate([own_rows[:, g * HD : (g + 1) * HD] for g in range(4)], axis=0)
    fresh = own_rows[:, 4 * HD : 6 * HD]
    parent = own_rows[TOKENS : TOKENS + 4, 0:HD].astype(F32)[0:1, 0:TOK]
    scaling = 1.0 / math.sqrt(HD)
    dims = (((1,), (1,)), ((), ()))
    reached = closure(parent)
    tree_mask = jnp.concatenate([reached] * 4, axis=0) > 0.5
    tree_score = lax.dot_general(q, fresh[:, 0:HD], dims, preferred_element_type=F32) * scaling
    tree_score = jnp.where(tree_mask, tree_score, NEG)
    peak = jnp.max(tree_score, axis=1, keepdims=True)
    scores = []
    for p in range(4):
        key = got[0:32, p].reshape(256, HD)
        score = lax.dot_general(q, key, dims, preferred_element_type=F32) * scaling
        seen = iota((4 * TOK, 256), 1) < length - p * 256
        score = jnp.where(seen, score, NEG)
        peak = jnp.maximum(peak, jnp.max(score, axis=1, keepdims=True))
        scores.append(score)
    expo = jnp.where(tree_mask, jnp.exp(tree_score - peak), 0.0)
    denom = jnp.sum(expo, axis=1, keepdims=True)
    numer = jnp.dot(expo.astype(BF16), fresh[:, HD : 2 * HD], preferred_element_type=F32)
    for p in range(4):
        seen = iota((4 * TOK, 256), 1) < length - p * 256
        expo = jnp.where(seen, jnp.exp(scores[p] - peak), 0.0)
        denom = denom + jnp.sum(expo, axis=1, keepdims=True)
        value = got[32:64, p].reshape(256, HD)
        numer = numer + jnp.dot(expo.astype(BF16), value, preferred_element_type=F32)
    attention = (numer / denom).astype(BF16)
    for m in range(8):
        out[m, 0 : 4 * TOK] = attention
        out[m, 4 * TOK : 4 * TOK + 8] = fresh_rows[m]


def append_body(owner, lens, path, cache, got, out, rows):
    slots = cache.shape[0]
    depth = path.shape[0]
    for s in range(slots):
        r = jnp.maximum(owner[0, s], 0)
        count = jnp.int32(0)
        for d in range(depth):
            count = count + jnp.where(path[d, r] >= 0, 1, 0)
        count = jnp.where(owner[0, s] >= 0, count, 0)
        first = lens[r] - owner[1, s] * 256
        for y in range(8):
            rows[2 * y : 2 * y + 2] = got[y, 4 * TOK : 4 * TOK + 8].astype(F32)[2 + 2 * s : 4 + 2 * s]
        fresh = jnp.concatenate([rows[0:8], rows[8:16]], axis=1).astype(BF16)
        pick = (iota((256, depth), 0) - first == iota((256, depth), 1)).astype(BF16)
        put = jnp.dot(pick, fresh, preferred_element_type=F32).astype(BF16)
        offset = iota((256, 2 * HD), 0) - first
        out[s] = jnp.where((offset >= 0) & (offset < count), put, cache[s])


def project_body(att, first_weight, last_weight, out):
    rows = 8 * TOKENS
    own = lax.axis_index("req")
    mine = (own % 2) * 4 + own // 16
    turned = (iota((rows, 256), 0) + 4 * (mine % 2) + 6) % 8
    pick = (iota((rows, 256), 1) == turned * TOK + iota((rows, 256), 0) // 8).astype(BF16)
    parts = [att[:, g * TOK : (g + 1) * TOK].reshape(256, HD) for g in range(4)]
    both = jnp.dot(pick, jnp.concatenate(parts, axis=1), preferred_element_type=F32).astype(BF16)
    half = rows // 2
    low = iota((half, HD), 1) < 64
    dims = (((1,), (1,)), ((), ()))
    for part, weight in enumerate((first_weight, last_weight)):
        product = lax.dot_general(both, weight[...].reshape(256, 512), dims, preferred_element_type=F32)
        for i in range(4):
            x = product[:, HD * (i // 2) : HD * (i // 2) + HD]
            if i % 2 == 0:
                block = jnp.where(low, x[0:half], pltpu.roll(x[half:rows], 64, 1))
            else:
                block = jnp.where(low, pltpu.roll(x[0:half], 64, 1), x[half:rows])
            out[mine ^ ORDER[4 * part + i]] = block.astype(BF16)


def total_body(got, out):
    acc = got[0].astype(F32)
    for k in range(1, 8):
        acc = acc + got[k].astype(F32)
    acc = acc.astype(BF16)
    half = TOKENS // 2
    out[0:half] = acc[:, 0:64].reshape(half, 8, 64)
    out[half:TOKENS] = acc[:, 64:128].reshape(half, 8, 64)


VM = pl.BlockSpec(memory_space=pltpu.VMEM)
SM = pl.BlockSpec(memory_space=pltpu.SMEM)


def near(x):
    return pltpu.with_memory_space_constraint(x, pltpu.VMEM)


def call(body, name, specs, out, scratch=()):
    return pl.pallas_call(
        body,
        name=name,
        in_specs=list(specs),
        out_specs=(VM,) * len(out) if isinstance(out, tuple) else VM,
        out_shape=out,
        scratch_shapes=list(scratch),
    )


def shards(queries, tree_kv, tree_parent, accepted_path, cache_kv, piece_owner, cache_len, out_weight):
    to_all = functools.partial(lax.all_to_all, split_axis=0, concat_axis=0, tiled=True)
    spot = [[16 * (a % 4) + 2 * b + a // 4 for b in range(8)] for a in range(8)]

    def swap(x, flip):
        return lax.ppermute(x, "req", [(spot[a][b], spot[a ^ flip][b]) for a in range(8) for b in range(8)])

    owner = piece_owner.T
    path = accepted_path.T
    with jax.named_scope("weight_gather"):
        one = out_weight.T[None]
        pair = jnp.concatenate([one, swap(one, 1)])
        other_pair = swap(pair, 4)
    with jax.named_scope("spread"):
        packed, own_rows = call(
            pack_body,
            "pack",
            (SM, SM, VM, VM, VM, VM),
            (jax.ShapeDtypeStruct((64, 4, 8, HD), BF16), jax.ShapeDtypeStruct((TOK, 6 * HD), BF16)),
            [pltpu.VMEM((8, HD), F32)],
        )(owner, path, cache_kv, queries, tree_kv, tree_parent)
        pieces = to_all(packed, "req")
        pieces, pair, other_pair, own_rows = lax.optimization_barrier((pieces, pair, other_pair, own_rows))
    with jax.named_scope("route"):
        routed, fresh_rows = call(
            route_body,
            "route",
            (VM,),
            (jax.ShapeDtypeStruct((64, 4, 8, HD), BF16), pltpu.VMEM((8, 8, HD), BF16)),
            [pltpu.VMEM((4, 256), jnp.int32), pltpu.SMEM((4, 256), jnp.int32), pltpu.SemaphoreType.DMA],
        )(near(pieces))
        home = to_all(routed, "req")
        first_weight = jnp.concatenate([pair, other_pair])
        last_weight = swap(first_weight, 3)
        moves = [(r, spot[r // 8][(r + 4 * (r // 8 % 2) + 6) % 8]) for r in range(64)]
        place_rows = lax.ppermute(own_rows, "req", moves)
        home, last_weight, place_rows = lax.optimization_barrier((home, last_weight, place_rows))
    with jax.named_scope("attend"):
        attention = call(attend_body, "attend", (SM, VM, VM, VM), pltpu.VMEM((8, 4 * TOK + 8, HD), BF16))(
            cache_len, near(place_rows), near(home), near(fresh_rows)
        )
        gathered = near(to_all(attention, "req", axis_index_groups=spot))
    with jax.named_scope("append"):
        cache_out = call(
            append_body,
            "append",
            (SM, SM, SM, VM, VM),
            jax.ShapeDtypeStruct(cache_kv.shape, BF16),
            [pltpu.VMEM((16, HD), F32)],
        )(owner, cache_len, path, cache_kv, gathered)
    with jax.named_scope("project"):
        partial = call(project_body, "project", (VM, VM, VM), pltpu.VMEM((8, 4 * TOKENS, HD), BF16))(
            gathered, near(first_weight), near(last_weight)
        )
        partials = to_all(partial, "tp")
        total = call(total_body, "total", (VM,), pltpu.VMEM((TOKENS, 8, 64), BF16))(near(partials))
        pairs = [(spot[a][b] * 8 + c, spot[c][b] * 8 + a) for a in range(8) for b in range(8) for c in range(8)]
        mixed = lax.ppermute(total, ("req", "tp"), pairs)
    return (mixed.transpose(1, 0, 2), cache_out)


def solution(mesh):
    return jax.shard_map(
        shards,
        mesh=mesh,
        in_specs=(
            P("req", None, "tp"),
            P("req", None, "tp"),
            P("req", None),
            P(),
            P("req", None, "tp"),
            P("req", None),
            P(),
            P("tp", "req"),
        ),
        out_specs=(P("tp", None, "req"), P("req", None, "tp")),
        check_vma=False,
    )
```

```python
import functools
import math

import jax
import jax.numpy as jnp
from jax import lax
from jax.experimental import pallas as pl
from jax.experimental.pallas import tpu as pltpu
from jax.sharding import PartitionSpec as P

HD = 128
NEG = -1e30
TOKENS = 28
TOK = 32
ORDER = (0, 1, 4, 5, 3, 2, 7, 6)
F32 = jnp.float32
BF16 = jnp.bfloat16


def iota(shape, dim):
    return lax.broadcasted_iota(jnp.int32, shape, dim)


def pack_body(owner, path, cache, query, tree, parent, out, rows, aux):
    slots = cache.shape[0]
    tokens = tree.shape[1]
    depth = path.shape[0]
    own = lax.axis_index("req")
    for s in range(slots):
        out[0:32, s] = cache[s, :, 0:HD].reshape(32, 8, HD)
        out[32:64, s] = cache[s, :, HD : 2 * HD].reshape(32, 8, HD)
    keys = jnp.full((8, HD), -1, jnp.int32)
    for s in range(slots):
        key = jnp.where(owner[0, s] >= 0, owner[0, s] * 4 + owner[1, s], -1)
        keys = jnp.where(iota((8, HD), 1) == s, key, keys)
    keyrow = jnp.where(iota((8, HD), 0) == 0, keys, 0).astype(F32)
    hot_col = iota((depth, tokens), 1)
    hot_row = iota((depth, tokens), 0)
    hot = jnp.zeros((depth, tokens), jnp.bool_)
    for d in range(depth):
        hot = hot | ((hot_row == d) & (hot_col == path[d, own]))
    fresh = jnp.dot(hot.astype(BF16), tree[0], preferred_element_type=F32)
    for y in range(8):
        aux[...] = keyrow
        two = fresh[2 * (y % 4) : 2 * (y % 4) + 2, HD * (y // 4) : HD * (y // 4) + HD]
        for i in range(slots):
            aux[2 + 2 * i : 4 + 2 * i] = two
        tile = aux[...].astype(BF16)
        for x in range(4):
            for core in range(2):
                out[16 * x + 2 * y + core, 3] = tile
    rows[...] = jnp.zeros_like(rows)
    rows[0:tokens, 0 : 4 * HD] = query[0]
    rows[0:tokens, 4 * HD : 6 * HD] = tree[0]
    rows[tokens : tokens + 1, 0:tokens] = parent[...].astype(F32).astype(BF16)


def route_body(got, out, fresh, table, table_s, sem, tiles, out_sem):
    own = lax.axis_index("req")
    keys = got[:, 3, 0:1, :].astype(F32).reshape(64, HD)
    source = iota((64, 256), 0)
    lane = iota((64, 256), 1)
    target = (place_request(lane // 4) * 4 + lane % 4).astype(F32)
    tile = (source * 4).astype(F32)
    diagonal = source == lane
    found = jnp.zeros((64, 256), F32)
    holders = []
    for i in range(3):
        key = keys[:, i : i + 1]
        found = found + jnp.where(key == target, tile + float(i), 0.0)
        request = jnp.floor(jnp.maximum(key, 0.0) * 0.25)
        holders.append(jnp.sum(jnp.where(diagonal, request, 0.0), axis=0, keepdims=True))
    found = jnp.minimum(jnp.sum(found, axis=0, keepdims=True), 255.0)
    table[...] = jnp.concatenate([found] + holders, axis=0).astype(jnp.int32)
    copy = pltpu.make_async_copy(table, table_s, sem)
    copy.start()
    copy.wait()

    def step(r, carry):
        for p in range(4):
            t = table_s[0, 4 * r + p]
            tiles[r, p] = got[t >> 2, t & 3]
        return carry

    copies = []
    for part in range(4):
        lax.fori_loop(16 * part, 16 * part + 16, step, 0, unroll=8)
        at = slice(16 * part, 16 * part + 16)
        copies.append(pltpu.make_async_copy(tiles.at[at], out.at[at], out_sem.at[part]))
        copies[-1].start()
    row = iota((8, HD), 0)
    for y in range(8):
        holder = (own // 16) * 16 + 2 * y + own % 2
        picks = [got[table_s[1 + i, holder], 3].astype(F32) for i in range(3)]
        fresh[y] = jnp.where(row < 4, picks[0], jnp.where(row < 6, picks[1], picks[2])).astype(BF16)
    for copy in copies:
        copy.wait()


def place_request(place):
    group = (place % 2) * 4 + place // 16
    return group * 8 + (place // 2 + 4 * (group % 2) + 2) % 8


def closure(parent):
    n = TOK
    up = iota((n, n), 0).astype(F32)
    here = iota((n, n), 1).astype(F32)
    eye = (up == here).astype(F32)
    reach = jnp.minimum((up == parent).astype(F32) + eye, 1.0)
    for rounds in range(5):
        low = reach.astype(BF16)
        reach = jnp.minimum(jnp.dot(low, low, preferred_element_type=F32), 1.0)
    return lax.dot_general(
        reach.astype(BF16), eye.astype(BF16), (((0,), (0,)), ((), ())), preferred_element_type=F32
    )


def attend_body(lens, own_rows, got, fresh_rows, out):
    length = lens[place_request(lax.axis_index("req"))]
    q = jnp.concatenate([own_rows[:, g * HD : (g + 1) * HD] for g in range(4)], axis=0)
    fresh = own_rows[:, 4 * HD : 6 * HD]
    parent = own_rows[TOKENS : TOKENS + 4, 0:HD].astype(F32)[0:1, 0:TOK]
    scaling = 1.0 / math.sqrt(HD)
    dims = (((1,), (1,)), ((), ()))
    reached = closure(parent)
    tree_mask = jnp.concatenate([reached] * 4, axis=0) > 0.5
    tree_score = lax.dot_general(q, fresh[:, 0:HD], dims, preferred_element_type=F32) * scaling
    tree_score = jnp.where(tree_mask, tree_score, NEG)
    peak = jnp.max(tree_score, axis=1, keepdims=True)
    scores = []
    for p in range(4):
        key = got[0:32, p].reshape(256, HD)
        score = lax.dot_general(q, key, dims, preferred_element_type=F32) * scaling
        seen = iota((4 * TOK, 256), 1) < length - p * 256
        score = jnp.where(seen, score, NEG)
        peak = jnp.maximum(peak, jnp.max(score, axis=1, keepdims=True))
        scores.append(score)
    expo = jnp.where(tree_mask, jnp.exp(tree_score - peak), 0.0)
    denom = jnp.sum(expo, axis=1, keepdims=True)
    numer = jnp.dot(expo.astype(BF16), fresh[:, HD : 2 * HD], preferred_element_type=F32)
    for p in range(4):
        seen = iota((4 * TOK, 256), 1) < length - p * 256
        expo = jnp.where(seen, jnp.exp(scores[p] - peak), 0.0)
        denom = denom + jnp.sum(expo, axis=1, keepdims=True)
        value = got[32:64, p].reshape(256, HD)
        numer = numer + jnp.dot(expo.astype(BF16), value, preferred_element_type=F32)
    attention = (numer / denom).astype(BF16)
    for m in range(8):
        out[m, 0 : 4 * TOK] = attention
        out[m, 4 * TOK : 4 * TOK + 8] = fresh_rows[m]


def append_body(owner, lens, path, cache, got, out, rows):
    slots = cache.shape[0]
    depth = path.shape[0]
    for s in range(slots):
        r = jnp.maximum(owner[0, s], 0)
        count = jnp.int32(0)
        for d in range(depth):
            count = count + jnp.where(path[d, r] >= 0, 1, 0)
        count = jnp.where(owner[0, s] >= 0, count, 0)
        first = lens[r] - owner[1, s] * 256
        for y in range(8):
            rows[2 * y : 2 * y + 2] = got[y, 4 * TOK : 4 * TOK + 8].astype(F32)[2 + 2 * s : 4 + 2 * s]
        fresh = jnp.concatenate([rows[0:8], rows[8:16]], axis=1).astype(BF16)
        pick = (iota((256, depth), 0) - first == iota((256, depth), 1)).astype(BF16)
        put = jnp.dot(pick, fresh, preferred_element_type=F32).astype(BF16)
        offset = iota((256, 2 * HD), 0) - first
        out[s] = jnp.where((offset >= 0) & (offset < count), put, cache[s])


def project_body(att, first_weight, last_weight, out):
    rows = 8 * TOKENS
    own = lax.axis_index("req")
    mine = (own % 2) * 4 + own // 16
    turned = (iota((rows, 256), 0) + 4 * (mine % 2) + 6) % 8
    pick = (iota((rows, 256), 1) == turned * TOK + iota((rows, 256), 0) // 8).astype(BF16)
    parts = [att[:, g * TOK : (g + 1) * TOK].reshape(256, HD) for g in range(4)]
    both = jnp.dot(pick, jnp.concatenate(parts, axis=1), preferred_element_type=F32).astype(BF16)
    half = rows // 2
    low = iota((half, HD), 1) < 64
    dims = (((1,), (1,)), ((), ()))
    for part, weight in enumerate((first_weight, last_weight)):
        product = lax.dot_general(both, weight[...].reshape(256, 512), dims, preferred_element_type=F32)
        for i in range(4):
            x = product[:, HD * (i // 2) : HD * (i // 2) + HD]
            if i % 2 == 0:
                block = jnp.where(low, x[0:half], pltpu.roll(x[half:rows], 64, 1))
            else:
                block = jnp.where(low, pltpu.roll(x[0:half], 64, 1), x[half:rows])
            out[mine ^ ORDER[4 * part + i]] = block.astype(BF16)


def total_body(got, out):
    acc = got[0].astype(F32)
    for k in range(1, 8):
        acc = acc + got[k].astype(F32)
    out[...] = acc.astype(BF16)


def place_body(got, out):
    half = TOKENS // 2
    out[0:half] = got[:, 0:64].reshape(half, 8, 64)
    out[half:TOKENS] = got[:, 64:128].reshape(half, 8, 64)


VM = pl.BlockSpec(memory_space=pltpu.VMEM)
SM = pl.BlockSpec(memory_space=pltpu.SMEM)
ANY = pl.BlockSpec(memory_space=pl.ANY)


def near(x):
    return pltpu.with_memory_space_constraint(x, pltpu.VMEM)


def call(body, name, specs, out, scratch=(), places=None):
    return pl.pallas_call(
        body,
        name=name,
        in_specs=list(specs),
        out_specs=places or ((VM,) * len(out) if isinstance(out, tuple) else VM),
        out_shape=out,
        scratch_shapes=list(scratch),
    )


def shards(queries, tree_kv, tree_parent, accepted_path, cache_kv, piece_owner, cache_len, out_weight):
    to_all = functools.partial(lax.all_to_all, split_axis=0, concat_axis=0, tiled=True)
    spot = [[16 * (a % 4) + 2 * b + a // 4 for b in range(8)] for a in range(8)]

    def swap(x, flip):
        return lax.ppermute(x, "req", [(spot[a][b], spot[a ^ flip][b]) for a in range(8) for b in range(8)])

    owner = piece_owner.T
    path = accepted_path.T
    with jax.named_scope("weight_gather"):
        one = out_weight.T[None]
        pair = jnp.concatenate([one, swap(one, 1)])
        other_pair = swap(pair, 4)
    with jax.named_scope("spread"):
        packed, own_rows = call(
            pack_body,
            "pack",
            (SM, SM, VM, VM, VM, VM),
            (jax.ShapeDtypeStruct((64, 4, 8, HD), BF16), jax.ShapeDtypeStruct((TOK, 6 * HD), BF16)),
            [pltpu.VMEM((8, HD), F32)],
        )(owner, path, cache_kv, queries, tree_kv, tree_parent)
        pieces = to_all(packed, "req")
        pieces, pair, other_pair, own_rows = lax.optimization_barrier((pieces, pair, other_pair, own_rows))
    with jax.named_scope("route"):
        routed, fresh_rows = call(
            route_body,
            "route",
            (VM,),
            (jax.ShapeDtypeStruct((64, 4, 8, HD), BF16), pltpu.VMEM((8, 8, HD), BF16)),
            [
                pltpu.VMEM((4, 256), jnp.int32),
                pltpu.SMEM((4, 256), jnp.int32),
                pltpu.SemaphoreType.DMA,
                pltpu.VMEM((64, 4, 8, HD), BF16),
                pltpu.SemaphoreType.DMA((4,)),
            ],
            (ANY, VM),
        )(near(pieces))
        home = to_all(routed, "req")
        first_weight = jnp.concatenate([pair, other_pair])
        last_weight = swap(first_weight, 3)
        moves = [(r, spot[r // 8][(r + 4 * (r // 8 % 2) + 6) % 8]) for r in range(64)]
        place_rows = lax.ppermute(own_rows, "req", moves)
        home, last_weight, place_rows = lax.optimization_barrier((home, last_weight, place_rows))
    with jax.named_scope("attend"):
        attention = call(attend_body, "attend", (SM, VM, VM, VM), pltpu.VMEM((8, 4 * TOK + 8, HD), BF16))(
            cache_len, near(place_rows), near(home), near(fresh_rows)
        )
        gathered = near(to_all(attention, "req", axis_index_groups=spot))
    with jax.named_scope("append"):
        cache_out = call(
            append_body,
            "append",
            (SM, SM, SM, VM, VM),
            jax.ShapeDtypeStruct(cache_kv.shape, BF16),
            [pltpu.VMEM((16, HD), F32)],
        )(owner, cache_len, path, cache_kv, gathered)
    with jax.named_scope("project"):
        partial = call(project_body, "project", (VM, VM, VM), pltpu.VMEM((8, 4 * TOKENS, HD), BF16))(
            gathered, near(first_weight), near(last_weight)
        )
        partials = to_all(partial, "tp")
        total = call(total_body, "total", (VM,), pltpu.VMEM((4 * TOKENS, HD), BF16))(near(partials))
        pairs = [(spot[a][b] * 8 + c, spot[c][b] * 8 + a) for a in range(8) for b in range(8) for c in range(8)]
        final = lax.ppermute(total, ("req", "tp"), pairs)
        mixed = call(place_body, "place", (VM,), jax.ShapeDtypeStruct((TOKENS, 8, 64), BF16))(near(final))
    return (mixed.transpose(1, 0, 2), cache_out)


def solution(mesh):
    return jax.shard_map(
        shards,
        mesh=mesh,
        in_specs=(
            P("req", None, "tp"),
            P("req", None, "tp"),
            P("req", None),
            P(),
            P("req", None, "tp"),
            P("req", None),
            P(),
            P("tp", "req"),
        ),
        out_specs=(P("tp", None, "req"), P("req", None, "tp")),
        check_vma=False,
    )
```

```python
import functools
import math

import jax
import jax.numpy as jnp
from jax import lax
from jax.experimental import pallas as pl
from jax.experimental.pallas import tpu as pltpu
from jax.sharding import PartitionSpec as P

HD = 128
NEG = -1e30
TOKENS = 28
TOK = 32
ORDER = (0, 1, 4, 5, 3, 2, 7, 6)
F32 = jnp.float32
BF16 = jnp.bfloat16


def iota(shape, dim):
    return lax.broadcasted_iota(jnp.int32, shape, dim)


def pack_body(owner, path, cache, query, tree, parent, out, rows, aux):
    slots = cache.shape[0]
    tokens = tree.shape[1]
    depth = path.shape[0]
    own = lax.axis_index("req")
    for s in range(slots):
        out[0:32, s] = cache[s, :, 0:HD].reshape(32, 8, HD)
        out[32:64, s] = cache[s, :, HD : 2 * HD].reshape(32, 8, HD)
    keys = jnp.full((8, HD), -1, jnp.int32)
    for s in range(slots):
        key = jnp.where(owner[0, s] >= 0, owner[0, s] * 4 + owner[1, s], -1)
        keys = jnp.where(iota((8, HD), 1) == s, key, keys)
    keyrow = jnp.where(iota((8, HD), 0) == 0, keys, 0).astype(F32)
    hot_col = iota((depth, tokens), 1)
    hot_row = iota((depth, tokens), 0)
    hot = jnp.zeros((depth, tokens), jnp.bool_)
    for d in range(depth):
        hot = hot | ((hot_row == d) & (hot_col == path[d, own]))
    fresh = jnp.dot(hot.astype(BF16), tree[0], preferred_element_type=F32)
    for y in range(8):
        aux[...] = keyrow
        two = fresh[2 * (y % 4) : 2 * (y % 4) + 2, HD * (y // 4) : HD * (y // 4) + HD]
        for i in range(slots):
            aux[2 + 2 * i : 4 + 2 * i] = two
        tile = aux[...].astype(BF16)
        for x in range(4):
            for core in range(2):
                out[16 * x + 2 * y + core, 3] = tile
    rows[...] = jnp.zeros_like(rows)
    rows[0:tokens, 0 : 4 * HD] = query[0]
    rows[0:tokens, 4 * HD : 6 * HD] = tree[0]
    rows[tokens : tokens + 1, 0:tokens] = parent[...].astype(F32).astype(BF16)


def route_body(got, out, fresh, table, table_s, sem, tiles, out_sem):
    own = lax.axis_index("req")
    keys = got[:, 3, 0:1, :].astype(F32).reshape(64, HD)
    source = iota((64, 256), 0)
    lane = iota((64, 256), 1)
    target = (place_request(lane // 4) * 4 + lane % 4).astype(F32)
    tile = (source * 4).astype(F32)
    diagonal = source == lane
    found = jnp.zeros((64, 256), F32)
    holders = []
    for i in range(3):
        key = keys[:, i : i + 1]
        found = found + jnp.where(key == target, tile + float(i), 0.0)
        request = jnp.floor(jnp.maximum(key, 0.0) * 0.25)
        holders.append(jnp.sum(jnp.where(diagonal, request, 0.0), axis=0, keepdims=True))
    found = jnp.minimum(jnp.sum(found, axis=0, keepdims=True), 255.0)
    table[...] = jnp.concatenate([found] + holders, axis=0).astype(jnp.int32)
    copy = pltpu.make_async_copy(table, table_s, sem)
    copy.start()
    copy.wait()

    def step(r, carry):
        for p in range(4):
            t = table_s[0, 4 * r + p]
            tiles[r, p] = got[t >> 2, t & 3]
        return carry

    copies = []
    for part in range(4):
        lax.fori_loop(16 * part, 16 * part + 16, step, 0, unroll=16)
        at = slice(16 * part, 16 * part + 16)
        copies.append(pltpu.make_async_copy(tiles.at[at], out.at[at], out_sem.at[part]))
        copies[-1].start()
    row = iota((8, HD), 0)
    for y in range(8):
        holder = (own // 16) * 16 + 2 * y + own % 2
        picks = [got[table_s[1 + i, holder], 3].astype(F32) for i in range(3)]
        fresh[y] = jnp.where(row < 4, picks[0], jnp.where(row < 6, picks[1], picks[2])).astype(BF16)
    for copy in copies:
        copy.wait()


def place_request(place):
    group = (place % 2) * 4 + place // 16
    return group * 8 + (place // 2 + 4 * (group % 2) + 2) % 8


def closure(parent):
    n = TOK
    up = iota((n, n), 0).astype(F32)
    here = iota((n, n), 1).astype(F32)
    eye = (up == here).astype(F32)
    reach = jnp.minimum((up == parent).astype(F32) + eye, 1.0)
    for rounds in range(5):
        low = reach.astype(BF16)
        reach = jnp.minimum(jnp.dot(low, low, preferred_element_type=F32), 1.0)
    return lax.dot_general(
        reach.astype(BF16), eye.astype(BF16), (((0,), (0,)), ((), ())), preferred_element_type=F32
    )


def attend_body(lens, own_rows, got, fresh_rows, out):
    length = lens[place_request(lax.axis_index("req"))]
    q = jnp.concatenate([own_rows[:, g * HD : (g + 1) * HD] for g in range(4)], axis=0)
    fresh = own_rows[:, 4 * HD : 6 * HD]
    parent = own_rows[TOKENS : TOKENS + 4, 0:HD].astype(F32)[0:1, 0:TOK]
    scaling = 1.0 / math.sqrt(HD)
    dims = (((1,), (1,)), ((), ()))
    reached = closure(parent)
    tree_mask = jnp.concatenate([reached] * 4, axis=0) > 0.5
    tree_score = lax.dot_general(q, fresh[:, 0:HD], dims, preferred_element_type=F32) * scaling
    tree_score = jnp.where(tree_mask, tree_score, NEG)
    peak = jnp.max(tree_score, axis=1, keepdims=True)
    scores = []
    for p in range(4):
        key = got[0:32, p].reshape(256, HD)
        score = lax.dot_general(q, key, dims, preferred_element_type=F32) * scaling
        seen = iota((4 * TOK, 256), 1) < length - p * 256
        score = jnp.where(seen, score, NEG)
        peak = jnp.maximum(peak, jnp.max(score, axis=1, keepdims=True))
        scores.append(score)
    expo = jnp.where(tree_mask, jnp.exp(tree_score - peak), 0.0)
    denom = jnp.sum(expo, axis=1, keepdims=True)
    numer = jnp.dot(expo.astype(BF16), fresh[:, HD : 2 * HD], preferred_element_type=F32)
    total = jnp.zeros((4 * TOK, 256), F32)
    for p in range(4):
        expo = jnp.exp(scores[p] - peak)
        total = total + expo
        value = got[32:64, p].reshape(256, HD)
        numer = numer + jnp.dot(expo.astype(BF16), value, preferred_element_type=F32)
    denom = denom + jnp.sum(total, axis=1, keepdims=True)
    attention = (numer / denom).astype(BF16)
    for m in range(8):
        out[m, 0 : 4 * TOK] = attention
        out[m, 4 * TOK : 4 * TOK + 8] = fresh_rows[m]


def append_body(owner, lens, path, cache, got, out, rows):
    slots = cache.shape[0]
    depth = path.shape[0]
    for s in range(slots):
        r = jnp.maximum(owner[0, s], 0)
        count = jnp.int32(0)
        for d in range(depth):
            count = count + jnp.where(path[d, r] >= 0, 1, 0)
        count = jnp.where(owner[0, s] >= 0, count, 0)
        first = lens[r] - owner[1, s] * 256
        for y in range(8):
            rows[2 * y : 2 * y + 2] = got[y, 4 * TOK : 4 * TOK + 8].astype(F32)[2 + 2 * s : 4 + 2 * s]
        fresh = jnp.concatenate([rows[0:8], rows[8:16]], axis=1).astype(BF16)
        pick = (iota((256, depth), 0) - first == iota((256, depth), 1)).astype(BF16)
        put = jnp.dot(pick, fresh, preferred_element_type=F32).astype(BF16)
        offset = iota((256, 2 * HD), 0) - first
        out[s] = jnp.where((offset >= 0) & (offset < count), put, cache[s])


def project_body(att, first_weight, last_weight, out):
    rows = 8 * TOKENS
    own = lax.axis_index("req")
    mine = (own % 2) * 4 + own // 16
    turned = (iota((rows, 256), 0) + 4 * (mine % 2) + 6) % 8
    pick = (iota((rows, 256), 1) == turned * TOK + iota((rows, 256), 0) // 8).astype(BF16)
    parts = [att[:, g * TOK : (g + 1) * TOK].reshape(256, HD) for g in range(4)]
    both = jnp.dot(pick, jnp.concatenate(parts, axis=1), preferred_element_type=F32).astype(BF16)
    half = rows // 2
    low = iota((half, HD), 1) < 64
    dims = (((1,), (1,)), ((), ()))
    for part, weight in enumerate((first_weight, last_weight)):
        product = lax.dot_general(both, weight[...].reshape(256, 512), dims, preferred_element_type=F32)
        for i in range(4):
            x = product[:, HD * (i // 2) : HD * (i // 2) + HD]
            if i % 2 == 0:
                block = jnp.where(low, x[0:half], pltpu.roll(x[half:rows], 64, 1))
            else:
                block = jnp.where(low, pltpu.roll(x[0:half], 64, 1), x[half:rows])
            out[mine ^ ORDER[4 * part + i]] = block.astype(BF16)


def total_body(got, out):
    acc = got[0].astype(F32)
    for k in range(1, 8):
        acc = acc + got[k].astype(F32)
    out[...] = acc.astype(BF16)


def place_body(got, out):
    half = TOKENS // 2
    out[0:half] = got[:, 0:64].reshape(half, 8, 64)
    out[half:TOKENS] = got[:, 64:128].reshape(half, 8, 64)


VM = pl.BlockSpec(memory_space=pltpu.VMEM)
SM = pl.BlockSpec(memory_space=pltpu.SMEM)
ANY = pl.BlockSpec(memory_space=pl.ANY)


def near(x):
    return pltpu.with_memory_space_constraint(x, pltpu.VMEM)


def call(body, name, specs, out, scratch=(), places=None):
    return pl.pallas_call(
        body,
        name=name,
        in_specs=list(specs),
        out_specs=places or ((VM,) * len(out) if isinstance(out, tuple) else VM),
        out_shape=out,
        scratch_shapes=list(scratch),
    )


def shards(queries, tree_kv, tree_parent, accepted_path, cache_kv, piece_owner, cache_len, out_weight):
    to_all = functools.partial(lax.all_to_all, split_axis=0, concat_axis=0, tiled=True)
    spot = [[16 * (a % 4) + 2 * b + a // 4 for b in range(8)] for a in range(8)]

    def swap(x, flip):
        return lax.ppermute(x, "req", [(spot[a][b], spot[a ^ flip][b]) for a in range(8) for b in range(8)])

    owner = piece_owner.T
    path = accepted_path.T
    with jax.named_scope("weight_gather"):
        one = out_weight.T[None]
        pair = jnp.concatenate([one, swap(one, 1)])
        other_pair = swap(pair, 4)
    with jax.named_scope("spread"):
        packed, own_rows = call(
            pack_body,
            "pack",
            (SM, SM, VM, VM, VM, VM),
            (jax.ShapeDtypeStruct((64, 4, 8, HD), BF16), jax.ShapeDtypeStruct((TOK, 6 * HD), BF16)),
            [pltpu.VMEM((8, HD), F32)],
        )(owner, path, cache_kv, queries, tree_kv, tree_parent)
        pieces = to_all(packed, "req")
        pieces, pair, other_pair, own_rows = lax.optimization_barrier((pieces, pair, other_pair, own_rows))
    with jax.named_scope("route"):
        routed, fresh_rows = call(
            route_body,
            "route",
            (VM,),
            (jax.ShapeDtypeStruct((64, 4, 8, HD), BF16), pltpu.VMEM((8, 8, HD), BF16)),
            [
                pltpu.VMEM((4, 256), jnp.int32),
                pltpu.SMEM((4, 256), jnp.int32),
                pltpu.SemaphoreType.DMA,
                pltpu.VMEM((64, 4, 8, HD), BF16),
                pltpu.SemaphoreType.DMA((4,)),
            ],
            (ANY, VM),
        )(near(pieces))
        home = to_all(routed, "req")
        first_weight = jnp.concatenate([pair, other_pair])
        last_weight = swap(first_weight, 3)
        moves = [(r, spot[r // 8][(r + 4 * (r // 8 % 2) + 6) % 8]) for r in range(64)]
        place_rows = lax.ppermute(own_rows, "req", moves)
        home, last_weight, place_rows = lax.optimization_barrier((home, last_weight, place_rows))
    with jax.named_scope("attend"):
        attention = call(attend_body, "attend", (SM, VM, VM, VM), pltpu.VMEM((8, 4 * TOK + 8, HD), BF16))(
            cache_len, near(place_rows), near(home), near(fresh_rows)
        )
        gathered = near(to_all(attention, "req", axis_index_groups=spot))
    with jax.named_scope("append"):
        cache_out = call(
            append_body,
            "append",
            (SM, SM, SM, VM, VM),
            jax.ShapeDtypeStruct(cache_kv.shape, BF16),
            [pltpu.VMEM((16, HD), F32)],
        )(owner, cache_len, path, cache_kv, gathered)
    with jax.named_scope("project"):
        partial = call(project_body, "project", (VM, VM, VM), pltpu.VMEM((8, 4 * TOKENS, HD), BF16))(
            gathered, near(first_weight), near(last_weight)
        )
        partials = to_all(partial, "tp")
        total = call(total_body, "total", (VM,), pltpu.VMEM((4 * TOKENS, HD), BF16))(near(partials))
        pairs = [(spot[a][b] * 8 + c, spot[c][b] * 8 + a) for a in range(8) for b in range(8) for c in range(8)]
        final = lax.ppermute(total, ("req", "tp"), pairs)
        mixed = call(place_body, "place", (VM,), jax.ShapeDtypeStruct((TOKENS, 8, 64), BF16))(near(final))
    return (mixed.transpose(1, 0, 2), cache_out)


def solution(mesh):
    return jax.shard_map(
        shards,
        mesh=mesh,
        in_specs=(
            P("req", None, "tp"),
            P("req", None, "tp"),
            P("req", None),
            P(),
            P("req", None, "tp"),
            P("req", None),
            P(),
            P("tp", "req"),
        ),
        out_specs=(P("tp", None, "req"), P("req", None, "tp")),
        check_vma=False,
    )
```

```python
import functools
import math

import jax
import jax.numpy as jnp
from jax import lax
from jax.experimental import pallas as pl
from jax.experimental.pallas import tpu as pltpu
from jax.sharding import PartitionSpec as P

HD = 128
NEG = -1e30
TOKENS = 28
TOK = 32
ORDER = (0, 1, 4, 5, 3, 2, 7, 6)
F32 = jnp.float32
BF16 = jnp.bfloat16


def iota(shape, dim):
    return lax.broadcasted_iota(jnp.int32, shape, dim)


def pack_body(owner, path, cache, query, tree, parent, out, rows, aux):
    slots = cache.shape[0]
    tokens = tree.shape[1]
    depth = path.shape[0]
    own = lax.axis_index("req")
    for s in range(slots):
        out[0:32, s] = cache[s, :, 0:HD].reshape(32, 8, HD)
        out[32:64, s] = cache[s, :, HD : 2 * HD].reshape(32, 8, HD)
    keys = jnp.full((8, HD), -1, jnp.int32)
    for s in range(slots):
        key = jnp.where(owner[0, s] >= 0, owner[0, s] * 4 + owner[1, s], -1)
        keys = jnp.where(iota((8, HD), 1) == s, key, keys)
    keyrow = jnp.where(iota((8, HD), 0) == 0, keys, 0).astype(F32)
    hot_col = iota((depth, tokens), 1)
    hot_row = iota((depth, tokens), 0)
    hot = jnp.zeros((depth, tokens), jnp.bool_)
    for d in range(depth):
        hot = hot | ((hot_row == d) & (hot_col == path[d, own]))
    fresh = jnp.dot(hot.astype(BF16), tree[0], preferred_element_type=F32)
    for y in range(8):
        aux[...] = keyrow
        two = fresh[2 * (y % 4) : 2 * (y % 4) + 2, HD * (y // 4) : HD * (y // 4) + HD]
        for i in range(slots):
            aux[2 + 2 * i : 4 + 2 * i] = two
        tile = aux[...].astype(BF16)
        for x in range(4):
            for core in range(2):
                out[16 * x + 2 * y + core, 3] = tile
    rows[...] = jnp.zeros_like(rows)
    rows[0:tokens, 0 : 4 * HD] = query[0]
    rows[0:tokens, 4 * HD : 6 * HD] = tree[0]
    rows[tokens : tokens + 1, 0:tokens] = parent[...].astype(F32).astype(BF16)


def route_body(got, out, fresh, table, table_s, sem, tiles, out_sem):
    own = lax.axis_index("req")
    keys = got[:, 3, 0:1, :].astype(F32).reshape(64, HD)
    source = iota((64, 256), 0)
    lane = iota((64, 256), 1)
    target = (place_request(lane // 4) * 4 + lane % 4).astype(F32)
    tile = (source * 4).astype(F32)
    diagonal = source[:, 0:HD] == lane[:, 0:HD]
    unused = jnp.zeros((1, HD), F32)
    found = jnp.zeros((64, 256), F32)
    holders = []
    for i in range(3):
        key = keys[:, i : i + 1]
        found = found + jnp.where(key == target, tile + float(i), 0.0)
        request = jnp.floor(jnp.maximum(key, 0.0) * 0.25)
        holder = jnp.sum(jnp.where(diagonal, request, 0.0), axis=0, keepdims=True)
        holders.append(jnp.concatenate([holder, unused], axis=1))
    found = jnp.minimum(jnp.sum(found, axis=0, keepdims=True), 255.0)
    table[...] = jnp.concatenate([found] + holders, axis=0).astype(jnp.int32)
    copy = pltpu.make_async_copy(table, table_s, sem)
    copy.start()
    copy.wait()

    def step(r, carry):
        for p in range(4):
            t = table_s[0, 4 * r + p]
            tiles[r, p] = got[t >> 2, t & 3]
        return carry

    copies = []
    for part in range(4):
        lax.fori_loop(16 * part, 16 * part + 16, step, 0, unroll=16)
        at = slice(16 * part, 16 * part + 16)
        copies.append(pltpu.make_async_copy(tiles.at[at], out.at[at], out_sem.at[part]))
        copies[-1].start()
    row = iota((8, HD), 0)
    for y in range(8):
        holder = (own // 16) * 16 + 2 * y + own % 2
        picks = [got[table_s[1 + i, holder], 3].astype(F32) for i in range(3)]
        fresh[y] = jnp.where(row < 4, picks[0], jnp.where(row < 6, picks[1], picks[2])).astype(BF16)
    for copy in copies:
        copy.wait()


def place_request(place):
    group = (place % 2) * 4 + place // 16
    return group * 8 + (place // 2 + 4 * (group % 2) + 2) % 8


def closure(parent):
    n = TOK
    up = iota((n, n), 0).astype(F32)
    here = iota((n, n), 1).astype(F32)
    eye = (up == here).astype(F32)
    reach = jnp.minimum((up == parent).astype(F32) + eye, 1.0)
    for rounds in range(5):
        low = reach.astype(BF16)
        reach = jnp.minimum(jnp.dot(low, low, preferred_element_type=F32), 1.0)
    return lax.dot_general(
        reach.astype(BF16), eye.astype(BF16), (((0,), (0,)), ((), ())), preferred_element_type=F32
    )


def attend_body(lens, own_rows, got, fresh_rows, out):
    length = lens[place_request(lax.axis_index("req"))]
    q = jnp.concatenate([own_rows[:, g * HD : (g + 1) * HD] for g in range(4)], axis=0)
    fresh = own_rows[:, 4 * HD : 6 * HD]
    parent = own_rows[TOKENS : TOKENS + 4, 0:HD].astype(F32)[0:1, 0:TOK]
    scaling = 1.0 / math.sqrt(HD)
    dims = (((1,), (1,)), ((), ()))
    reached = closure(parent)
    tree_mask = jnp.concatenate([reached] * 4, axis=0) > 0.5
    tree_score = lax.dot_general(q, fresh[:, 0:HD], dims, preferred_element_type=F32) * scaling
    tree_score = jnp.where(tree_mask, tree_score, NEG)
    peak = jnp.max(tree_score, axis=1, keepdims=True)
    scores = []
    for p in range(4):
        key = got[0:32, p].reshape(256, HD)
        score = lax.dot_general(q, key, dims, preferred_element_type=F32) * scaling
        seen = iota((4 * TOK, 256), 1) < length - p * 256
        score = jnp.where(seen, score, NEG)
        peak = jnp.maximum(peak, jnp.max(score, axis=1, keepdims=True))
        scores.append(score)
    expo = jnp.where(tree_mask, jnp.exp(tree_score - peak), 0.0)
    denom = jnp.sum(expo, axis=1, keepdims=True)
    numer = jnp.dot(expo.astype(BF16), fresh[:, HD : 2 * HD], preferred_element_type=F32)
    total = jnp.zeros((4 * TOK, 256), F32)
    for p in range(4):
        expo = jnp.exp(scores[p] - peak)
        total = total + expo
        value = got[32:64, p].reshape(256, HD)
        numer = numer + jnp.dot(expo.astype(BF16), value, preferred_element_type=F32)
    denom = denom + jnp.sum(total, axis=1, keepdims=True)
    attention = (numer / denom).astype(BF16)
    for m in range(8):
        out[m, 0 : 4 * TOK] = attention
        out[m, 4 * TOK : 4 * TOK + 8] = fresh_rows[m]


def append_body(owner, lens, path, cache, got, out, rows):
    slots = cache.shape[0]
    depth = path.shape[0]
    for s in range(slots):
        r = jnp.maximum(owner[0, s], 0)
        count = jnp.int32(0)
        for d in range(depth):
            count = count + jnp.where(path[d, r] >= 0, 1, 0)
        count = jnp.where(owner[0, s] >= 0, count, 0)
        first = lens[r] - owner[1, s] * 256
        for y in range(8):
            rows[2 * y : 2 * y + 2] = got[y, 4 * TOK : 4 * TOK + 8].astype(F32)[2 + 2 * s : 4 + 2 * s]
        fresh = jnp.concatenate([rows[0:8], rows[8:16]], axis=1).astype(BF16)
        pick = (iota((256, depth), 0) - first == iota((256, depth), 1)).astype(BF16)
        put = jnp.dot(pick, fresh, preferred_element_type=F32).astype(BF16)
        offset = iota((256, 2 * HD), 0) - first
        out[s] = jnp.where((offset >= 0) & (offset < count), put, cache[s])


def project_body(att, first_weight, last_weight, out):
    rows = 8 * TOKENS
    own = lax.axis_index("req")
    mine = (own % 2) * 4 + own // 16
    turned = (iota((rows, 256), 0) + 4 * (mine % 2) + 6) % 8
    pick = (iota((rows, 256), 1) == turned * TOK + iota((rows, 256), 0) // 8).astype(BF16)
    parts = [att[:, g * TOK : (g + 1) * TOK].reshape(256, HD) for g in range(4)]
    both = jnp.dot(pick, jnp.concatenate(parts, axis=1), preferred_element_type=F32).astype(BF16)
    half = rows // 2
    low = iota((half, HD), 1) < 64
    dims = (((1,), (1,)), ((), ()))
    for part, weight in enumerate((first_weight, last_weight)):
        product = lax.dot_general(both, weight[...].reshape(256, 512), dims, preferred_element_type=F32)
        for i in range(4):
            x = product[:, HD * (i // 2) : HD * (i // 2) + HD]
            if i % 2 == 0:
                block = jnp.where(low, x[0:half], pltpu.roll(x[half:rows], 64, 1))
            else:
                block = jnp.where(low, pltpu.roll(x[0:half], 64, 1), x[half:rows])
            out[mine ^ ORDER[4 * part + i]] = block.astype(BF16)


def total_body(got, out):
    acc = got[0].astype(F32)
    for k in range(1, 8):
        acc = acc + got[k].astype(F32)
    out[...] = acc.astype(BF16)


def place_body(got, out):
    half = TOKENS // 2
    out[0:half] = got[:, 0:64].reshape(half, 8, 64)
    out[half:TOKENS] = got[:, 64:128].reshape(half, 8, 64)


VM = pl.BlockSpec(memory_space=pltpu.VMEM)
SM = pl.BlockSpec(memory_space=pltpu.SMEM)
ANY = pl.BlockSpec(memory_space=pl.ANY)


def near(x):
    return pltpu.with_memory_space_constraint(x, pltpu.VMEM)


def call(body, name, specs, out, scratch=(), places=None):
    return pl.pallas_call(
        body,
        name=name,
        in_specs=list(specs),
        out_specs=places or ((VM,) * len(out) if isinstance(out, tuple) else VM),
        out_shape=out,
        scratch_shapes=list(scratch),
    )


def shards(queries, tree_kv, tree_parent, accepted_path, cache_kv, piece_owner, cache_len, out_weight):
    to_all = functools.partial(lax.all_to_all, split_axis=0, concat_axis=0, tiled=True)
    spot = [[16 * (a % 4) + 2 * b + a // 4 for b in range(8)] for a in range(8)]

    def swap(x, flip):
        return lax.ppermute(x, "req", [(spot[a][b], spot[a ^ flip][b]) for a in range(8) for b in range(8)])

    owner = piece_owner.T
    path = accepted_path.T
    with jax.named_scope("weight_gather"):
        one = out_weight.T[None]
        pair = jnp.concatenate([one, swap(one, 1)])
        other_pair = swap(pair, 4)
    with jax.named_scope("spread"):
        packed, own_rows = call(
            pack_body,
            "pack",
            (SM, SM, VM, VM, VM, VM),
            (jax.ShapeDtypeStruct((64, 4, 8, HD), BF16), jax.ShapeDtypeStruct((TOK, 6 * HD), BF16)),
            [pltpu.VMEM((8, HD), F32)],
        )(owner, path, cache_kv, queries, tree_kv, tree_parent)
        pieces = to_all(packed, "req")
        pieces, pair, other_pair, own_rows = lax.optimization_barrier((pieces, pair, other_pair, own_rows))
    with jax.named_scope("route"):
        routed, fresh_rows = call(
            route_body,
            "route",
            (VM,),
            (jax.ShapeDtypeStruct((64, 4, 8, HD), BF16), pltpu.VMEM((8, 8, HD), BF16)),
            [
                pltpu.VMEM((4, 256), jnp.int32),
                pltpu.SMEM((4, 256), jnp.int32),
                pltpu.SemaphoreType.DMA,
                pltpu.VMEM((64, 4, 8, HD), BF16),
                pltpu.SemaphoreType.DMA((4,)),
            ],
            (ANY, VM),
        )(near(pieces))
        home = to_all(routed, "req")
        first_weight = jnp.concatenate([pair, other_pair])
        last_weight = swap(first_weight, 3)
        moves = [(r, spot[r // 8][(r + 4 * (r // 8 % 2) + 6) % 8]) for r in range(64)]
        place_rows = lax.ppermute(own_rows, "req", moves)
        home, last_weight, place_rows = lax.optimization_barrier((home, last_weight, place_rows))
    with jax.named_scope("attend"):
        attention = call(attend_body, "attend", (SM, VM, VM, VM), pltpu.VMEM((8, 4 * TOK + 8, HD), BF16))(
            cache_len, near(place_rows), near(home), near(fresh_rows)
        )
        gathered = near(to_all(attention, "req", axis_index_groups=spot))
    with jax.named_scope("append"):
        cache_out = call(
            append_body,
            "append",
            (SM, SM, SM, VM, VM),
            jax.ShapeDtypeStruct(cache_kv.shape, BF16),
            [pltpu.VMEM((16, HD), F32)],
        )(owner, cache_len, path, cache_kv, gathered)
    with jax.named_scope("project"):
        partial = call(project_body, "project", (VM, VM, VM), pltpu.VMEM((8, 4 * TOKENS, HD), BF16))(
            gathered, near(first_weight), near(last_weight)
        )
        partials = to_all(partial, "tp")
        total = call(total_body, "total", (VM,), pltpu.VMEM((4 * TOKENS, HD), BF16))(near(partials))
        pairs = [(spot[a][b] * 8 + c, spot[c][b] * 8 + a) for a in range(8) for b in range(8) for c in range(8)]
        final = lax.ppermute(total, ("req", "tp"), pairs)
        mixed = call(place_body, "place", (VM,), jax.ShapeDtypeStruct((TOKENS, 8, 64), BF16))(near(final))
    return (mixed.transpose(1, 0, 2), cache_out)


def solution(mesh):
    return jax.shard_map(
        shards,
        mesh=mesh,
        in_specs=(
            P("req", None, "tp"),
            P("req", None, "tp"),
            P("req", None),
            P(),
            P("req", None, "tp"),
            P("req", None),
            P(),
            P("tp", "req"),
        ),
        out_specs=(P("tp", None, "req"), P("req", None, "tp")),
        check_vma=False,
    )
```
